256 devices in a mesh: row: 8 (over x_hi, y), col: 32 (over z, x_lo, core).
Axes of the slice: x: 4 (x_hi: 2, x_lo: 2; x = x_hi * 2 + x_lo), y: 4, z: 8, core: 2. Of those that a mesh axis runs over, the one named last changes fastest.
Arguments:
- feats: bfloat16 [32, 1024, 512], P('col', 'row'), may hold values from -6 to 6
- weight: bfloat16 [512, 512], replicated, may hold values from -0.25 to 0.25
- cotangent: bfloat16 [8, 4096, 512], P('row', 'col'), may hold values from -6 to 6
- tile_values: bfloat16 [8, 32, 96, 128, 128], P('row', 'col'), may hold values from -0.078125 to 0.078125
- tile_rows: int32 [8, 32, 96], P('row', 'col'), may hold values from 0 to 31, as said below
- tile_cols: int32 [8, 32, 96], P('row', 'col'), may hold values from 0 to 7, as said below
- tile_count: int32 [8, 32], P('row', 'col'), may hold values from 1 to 96, as said below
Outputs:
- layer_out: bfloat16 [8, 4096, 512], P('row', 'col')
- feat_grad: bfloat16 [32, 1024, 512], P('col', 'row')
- weight_grad: float32 [512, 512], replicated
The draws below stay inside these ranges and needn't reach their ends.
Inputs may be any that keep to these rules, and one draw needn't show every extreme that they name: `tile_rows`: with tile_cols, the tile coordinates of each block's listed tiles; no tile appears twice in a block's list. `tile_cols`: with tile_rows, the tile coordinates of each block's listed tiles. `tile_count`: slots at or beyond a block's count are unused; some block lists exactly 96 tiles.
All inputs are finite; a program needn't handle non-finite values.
Results may differ from the reference program's by a relative error of at most 0.024.
Values may be sent and summed in bfloat16 or wider, within the bound.
A program may use at most 128 MiB of HBM per device.

```python
import jax
import jax.numpy as jnp
from jax import lax

F = 512
TILE = 128
NODES = 32768
ROW_PANEL = 4096
COL_PANEL = 1024
ROW_TILES = 32
COL_TILES = 8
TILE_SLOTS = 96
N_ROW = 8
N_COL = 32


def tile_layout(key):
    block_keys = jax.random.split(jax.random.fold_in(key, 11), N_ROW * N_COL)

    def one_block(block_key):
        return jax.random.permutation(block_key, ROW_TILES * COL_TILES)[:TILE_SLOTS]
    chosen = jax.vmap(one_block)(block_keys).astype(jnp.int32)
    return chosen.reshape(N_ROW, N_COL, TILE_SLOTS)


def draw_tile_rows(key, part):
    return (tile_layout(key) // COL_TILES).astype(jnp.int32)


def draw_tile_cols(key, part):
    return (tile_layout(key) % COL_TILES).astype(jnp.int32)


def draw_tile_count(key, part):
    halvings = jax.random.randint(jax.random.fold_in(key, 13), (N_ROW * N_COL,), 0, 4).astype(jnp.int32)
    divisor = jnp.left_shift(jnp.ones_like(halvings), halvings)
    counted = jnp.maximum(TILE_SLOTS // divisor, 1).astype(jnp.int32)
    forced = jax.random.randint(jax.random.fold_in(key, 17), (), 0, N_ROW * N_COL)
    counted = counted.at[forced].set(TILE_SLOTS)
    return counted.reshape(N_ROW, N_COL).astype(jnp.int32)


def steps_of(key, dims, shards, low, largest):
    level = 1.0
    for axis_at, shards_of in shards:
        draws = jax.random.uniform(jax.random.fold_in(jax.random.fold_in(key, 6), axis_at), (shards_of,), jnp.float32, low / len(shards), largest / len(shards))
        level = level * jnp.repeat(jnp.exp(draws), dims[axis_at] // shards_of).reshape((-1,) + (1,) * (len(dims) - 1 - axis_at))
    return level


def scatter_about(stream_key, shape, scale, limit, pieces=(), held_as=jnp.bfloat16):
    entries = jax.random.normal(stream_key, shape, jnp.float32) * scale
    if len(pieces) > 0:
        entries = steps_of(stream_key, shape, pieces, -0.22, 0.18) * entries
    return jnp.clip(entries, min=-limit, max=limit).astype(held_as)


def setup_inputs(seed: int = 0) -> dict:
    streams_of = jax.random.split(jax.random.key(seed), 8)
    return {
        "feats": scatter_about(streams_of[0], (N_COL, COL_PANEL, F), 1.0, 6.0, ((0, 32), (1, 8))),
        "weight": scatter_about(streams_of[1], (F, F), F ** -0.5, 0.25),
        "cotangent": scatter_about(streams_of[2], (N_ROW, ROW_PANEL, F), 1.0, 6.0, ((0, 8), (1, 32))),
        "tile_values": scatter_about(streams_of[3], (N_ROW, N_COL, TILE_SLOTS, TILE, TILE), (TILE_SLOTS * N_COL * 128 // (2 * ROW_TILES)) ** -0.5, 0.078125, ((0, 8), (1, 32))),
        "tile_rows": draw_tile_rows(jax.random.fold_in(streams_of[7], 71), 0),
        "tile_cols": draw_tile_cols(jax.random.fold_in(streams_of[7], 71), 0),
        "tile_count": draw_tile_count(jax.random.fold_in(streams_of[7], 71), 0),
    }


def reference(feats, weight, cotangent, tile_values, tile_rows, tile_cols, tile_count):
    feature_width = feats.shape[2]
    panels = feats.reshape(N_COL, COL_TILES, 128, feature_width)
    slot_ids = jnp.arange(TILE_SLOTS, dtype=jnp.int32)
    block_ids = jnp.arange(N_ROW * N_COL, dtype=jnp.int32)

    def forward_block(running, block_index):
        block_row = block_index // N_COL
        block_col = block_index % N_COL
        keep_mask = (slot_ids < tile_count[block_row, block_col]).astype(jnp.float32)
        tiles_now = tile_values[block_row, block_col].astype(jnp.float32) * keep_mask[:, None, None]
        picked = panels[block_col][tile_cols[block_row, block_col]].astype(jnp.float32)
        products = jnp.einsum("gab,gbf->gaf", tiles_now, picked)
        row_part = jnp.zeros((ROW_TILES, 128, feature_width), jnp.float32).at[tile_rows[block_row, block_col]].add(products)
        row_part = lax.optimization_barrier(row_part.astype(jnp.bfloat16)).astype(jnp.float32)
        return running.at[block_row].add(row_part), None

    start_sum = jnp.zeros((N_ROW, ROW_TILES, 128, feature_width), jnp.float32)
    summed, _ = lax.scan(forward_block, start_sum, block_ids)
    summed_bf = summed.reshape(N_ROW * ROW_TILES * 128, feature_width).astype(jnp.bfloat16)
    hidden = jnp.dot(summed_bf, weight, preferred_element_type=jnp.float32)
    sigmoid_part = jax.nn.sigmoid(hidden)
    layer_out = (hidden * sigmoid_part).astype(jnp.bfloat16).reshape(N_ROW, ROW_TILES * 128, feature_width)
    hidden_grad = (cotangent.reshape(-1, feature_width).astype(jnp.float32) * sigmoid_part * (1.0 + hidden * (1.0 - sigmoid_part))).astype(jnp.bfloat16)
    grad_rows = lax.dot_general(hidden_grad, weight, (((1,), (1,)), ((), ())), preferred_element_type=jnp.float32).astype(jnp.bfloat16)
    weight_grad = lax.dot_general(summed_bf, hidden_grad, (((0,), (0,)), ((), ())), preferred_element_type=jnp.float32) * (NODES ** -0.5)
    grad_tiles = grad_rows.reshape(N_ROW, ROW_TILES, 128, feature_width)

    def backward_block(running, block_index):
        block_row = block_index // N_COL
        block_col = block_index % N_COL
        keep_mask = (slot_ids < tile_count[block_row, block_col]).astype(jnp.float32)
        tiles_now = tile_values[block_row, block_col].astype(jnp.float32) * keep_mask[:, None, None]
        picked = grad_tiles[block_row][tile_rows[block_row, block_col]].astype(jnp.float32)
        products = jnp.einsum("gab,gaf->gbf", tiles_now, picked)
        block_part = jnp.zeros((COL_TILES, 128, feature_width), jnp.float32).at[tile_cols[block_row, block_col]].add(products)
        block_part = lax.optimization_barrier(block_part.astype(jnp.bfloat16)).astype(jnp.float32)
        return running.at[block_col].add(block_part), None

    start_grad = jnp.zeros((N_COL, COL_TILES, 128, feature_width), jnp.float32)
    grad_sum, _ = lax.scan(backward_block, start_grad, block_ids)
    feat_grad = grad_sum.reshape(N_COL, COL_TILES * 128, feature_width).astype(jnp.bfloat16)
    return layer_out, feat_grad, weight_grad
```

```python
import functools

import jax
import jax.numpy as jnp
from jax import lax
from jax.experimental import pallas as pl
from jax.experimental.pallas import tpu as pltpu
from jax.sharding import PartitionSpec as P

BF = jnp.bfloat16
F32 = jnp.float32
X_HI, X_LO, CORE = 2, 2, 2


def layer_kernel(
    n_row, n_col, tab, feats, weight, cot, tiles_hbm, layer_out, feat_grad, weight_grad,
    tiles, dense, panel, part, core_in, rp, rm, own_sum, x_in, gath, acc, back, yp, ym, xb_in,
    w_term, w_core, wy_p, wy_m, w_y, wx_p, wx_m, w_x, w_z,
    tile_sem, send_sems, recv_sems, core_send, core_recv,
):
    Y, Z = n_row // X_HI, n_col // (X_LO * CORE)
    X = X_HI * X_LO
    HZ = Z // 2
    slots = tiles_hbm.shape[0]
    row_tiles, col_tiles = tab.shape
    chunk = row_tiles * 128 // Z
    width = feats.shape[1]

    r, c = lax.axis_index("row"), lax.axis_index("col")
    xh, y = r // Y, r % Y
    z, xl, k = c // (X_LO * CORE), (c // CORE) % X_LO, c % CORE
    x = xh * X_LO + xl

    def device(x_at, y_at, z_at, k_at):
        return ((x_at // X_LO) * Y + y_at, z_at * (X_LO * CORE) + (x_at % X_LO) * CORE + k_at)

    core_dev = device(x, y, z, 1 - k)
    x_plus, x_minus = device((x + 1) % X, y, z, k), device((x + X - 1) % X, y, z, k)
    x_far = device((x + 2) % X, y, z, k)
    x_near = device(xh * X_LO + 1 - xl, y, z, k)
    y_plus, y_minus = device(x, (y + 1) % Y, z, k), device(x, (y + Y - 1) % Y, z, k)
    z_plus, z_minus = device(x, y, (z + 1) % Z, k), device(x, y, (z + Z - 1) % Z, k)

    pending = []
    counters = {"send": 0, "recv": 0}

    def fresh():
        counters["recv"] += 1
        return counters["recv"] - 1

    def remote(src, dst, sem_out, sem_in, dev):
        return pltpu.make_async_remote_copy(
            src_ref=src, dst_ref=dst, send_sem=sem_out, recv_sem=sem_in,
            device_id=dev, device_id_type=pl.DeviceIdType.MESH,
        )

    def send(src, dst, sem, dev):
        copy = remote(src, dst, send_sems.at[counters["send"]], recv_sems.at[sem], dev)
        counters["send"] += 1
        copy.start()
        pending.append(copy)

    def arrived(view, sem):
        remote(view, view, send_sems.at[0], recv_sems.at[sem], core_dev).wait_recv()

    def add_into(dst, other):
        dst[...] = (dst[...].astype(F32) + other[...].astype(F32)).astype(dst.dtype)

    def ring_gather(pos, n, view, plus, minus, ready=None, on_block=None):
        half = n // 2
        sems = {(s, d, o): fresh() for s in (1, -1) for d in range(1, half + 1) for o in (0, 1)}

        def goes(s, d, o):
            return d < half or (d == half and o == (0 if s == 1 else 1))

        for o in (0, 1):
            if ready is not None:
                ready(o)
            for s in (1, -1):
                if goes(s, 1, o):
                    send(view(pos, o), view(pos, o), sems[s, 1, o], plus if s == 1 else minus)
        for d in range(1, half + 1):
            yield
            for o in (0, 1):
                for s in (1, -1):
                    if not goes(s, d, o):
                        continue
                    at = (pos - s * d + n) % n
                    arrived(view(at, o), sems[s, d, o])
                    if goes(s, d + 1, o):
                        send(view(at, o), view(at, o), sems[s, d + 1, o], plus if s == 1 else minus)
                    if on_block is not None:
                        on_block(at, o, s, d)

    def ring_sum(pos, n, view, bufs_p, bufs_m, plus, minus, before=None):
        half = n // 2
        bufs, dev = {1: bufs_p, -1: bufs_m}, {1: plus, -1: minus}
        sems = {(s, d, o): fresh() for s in (1, -1) for d in range(half) for o in (0, 1)}
        first = {(1, 0): half, (1, 1): half - 1, (-1, 1): half, (-1, 0): half - 1}
        for o in (0, 1):
            for s in (1, -1):
                d = first[s, o]
                if d > 0 and d == half:
                    send(view((pos + s * d + n) % n, o), bufs[s].at[d - 1, o], sems[s, d - 1, o], dev[s])
        for o in (1, 0):
            for s in (1, -1):
                d = first[s, o]
                if d > 0 and d < half:
                    send(view((pos + s * d + n) % n, o), bufs[s].at[d - 1, o], sems[s, d - 1, o], dev[s])
        for d in range(half - 1, 0, -1):
            yield
            if before is not None:
                before(d)
            for o in (1, 0):
                for s in (1, -1):
                    if d >= first[s, o]:
                        continue
                    buf = bufs[s].at[d, o]
                    arrived(buf, sems[s, d, o])
                    add_into(buf, view((pos + s * d + n) % n, o))
                    send(buf, bufs[s].at[d - 1, o], sems[s, d - 1, o], dev[s])
        yield
        if before is not None:
            before(0)

        def total(o):
            value = view(pos, o)[...].astype(F32)
            for s in (1, -1):
                if first[s, o] > 0:
                    arrived(bufs[s].at[0, o], sems[s, 0, o])
                    value = value + bufs[s][0, o].astype(F32)
            return value

        return total

    tile_copy = pltpu.make_async_copy(tiles_hbm, tiles.at[pl.ds(0, slots)], tile_sem)
    tile_copy.start()
    barrier = pltpu.get_barrier_semaphore()
    peers = (core_dev, x_plus, x_minus, x_far, y_plus, y_minus, z_plus, z_minus)
    for dev in peers:
        pl.semaphore_signal(barrier, inc=1, device_id=dev, device_id_type=pl.DeviceIdType.MESH)
    tiles[slots] = jnp.zeros(tiles.shape[1:], tiles.dtype)
    pl.semaphore_wait(barrier, len(peers))

    def panel_at(at, o):
        return panel.at[(xh if o == 0 else 1 - xh) * Y + at]

    panel[xh * Y + y] = feats[...]
    far_sem = fresh()
    send(feats, panel_at(y, 0), far_sem, x_far)

    def densify():
        tile_copy.wait()

        def one_row(i, carry):
            for j in range(col_tiles):
                dense[pl.ds(pl.multiple_of(i * 128, 128), 128), j * 128 : (j + 1) * 128] = tiles[tab[i, j]]
            return carry

        lax.fori_loop(0, row_tiles, one_row, 0)

    def panel_ready(o):
        if o == 1:
            densify()
            arrived(panel_at(y, 1), far_sem)

    for _ in ring_gather(y, Y, panel_at, y_plus, y_minus, ready=panel_ready):
        pass

    def forward_chunk(t, carry):
        off = HZ + (1 - 2 * (t % 2)) * ((t + 1) // 2)
        at = (z + off) % Z
        product = jnp.dot(
            dense[pl.ds(pl.multiple_of(at * chunk, chunk), chunk), :],
            panel[...].reshape(col_tiles * 128, width),
            preferred_element_type=F32,
        )
        part[at] = product.astype(BF).reshape(X_LO, CORE, 128, width)
        remote(
            part.at[at, :, 1 - k], core_in.at[at], core_send.at[t], core_recv.at[t], core_dev
        ).start()
        return carry

    def core_total(t):
        off = HZ + (1 - 2 * (t % 2)) * ((t + 1) // 2)
        at = (z + off) % Z
        remote(
            part.at[at, :, 1 - k], core_in.at[at], core_send.at[t], core_recv.at[t], core_dev
        ).wait()
        for o in range(X_LO):
            add_into(core_in.at[at, o], part.at[at, o, k])

    def sum_at(at, o):
        return core_in.at[at, xl if o == 0 else 1 - xl]

    lax.fori_loop(0, 3, forward_chunk, 0)
    for t in range(3):
        core_total(t)

    done = [3]

    def before(d):
        if d == HZ - 1:
            lax.fori_loop(3, Z, forward_chunk, 0)
        while done[0] < Z and d <= HZ - 2 and done[0] <= 2 * (HZ - d):
            core_total(done[0])
            done[0] += 1

    steps = ring_sum(z, Z, sum_at, rp, rm, z_plus, z_minus, before=before)
    while True:
        try:
            next(steps)
        except StopIteration as stop:
            total = stop.value
            break
    x_sem = fresh()
    own_sum[...] = total(1).astype(BF)
    send(own_sum, x_in, x_sem, x_near)
    mine = total(0)
    arrived(x_in, x_sem)
    summed = (mine + x_in[...].astype(F32)).astype(BF)

    hidden = jnp.dot(summed, weight[...], preferred_element_type=F32)
    gate = jax.nn.sigmoid(hidden)
    hidden_grad = (cot[...].astype(F32) * gate * (1.0 + hidden * (1.0 - gate))).astype(BF)
    grad_rows = lax.dot_general(
        hidden_grad, weight[...], (((1,), (1,)), ((), ())), preferred_element_type=F32
    ).astype(BF)
    gath[z, xl, k] = grad_rows

    near_sem = fresh()

    def gath_at(at, o):
        return gath.at[at, xl if o == 0 else 1 - xl, k]

    def gath_other(at, o):
        return gath.at[at, xl if o == 0 else 1 - xl, 1 - k]

    pair_sems = {}

    def to_core(at, o, s, d):
        key = (o, s, d)
        pair_sems[key] = fresh()
        send(gath_at(at, o), gath_at(at, o), pair_sems[key], core_dev)

    send(gath_at(z, 0), gath_at(z, 0), near_sem, x_near)

    def gath_ready(o):
        if o == 1:
            to_core(z, 0, 1, 0)
            layer_out[...] = (hidden * gate).astype(BF)
            w_term[...] = (
                lax.dot_general(summed, hidden_grad, (((0,), (0,)), ((), ())), preferred_element_type=F32)
                * (n_row * n_col * 128) ** (-0.5)
            ).reshape(w_term.shape)
            arrived(gath_at(z, 1), near_sem)

    def backward_chunk(at):
        product = lax.dot_general(
            dense[pl.ds(pl.multiple_of(at * chunk, chunk), chunk), :],
            gath[at].reshape(chunk, width),
            (((0,), (0,)), ((), ())),
            preferred_element_type=F32,
        )
        return product

    def accumulate(keys, at, start=False):
        for o, s, d in keys:
            arrived(gath_other(at, o), pair_sems[o, s, d])
        if start:
            acc[...] = backward_chunk(at)
        else:
            acc[...] += backward_chunk(at)

    def weight_steps():
        sem = fresh()
        send(w_term.at[1 - k], w_core, sem, core_dev)
        yield
        arrived(w_core, sem)
        add_into(w_core, w_term.at[k])
        total = yield from ring_sum(
            y, Y, lambda at, o: w_core.at[at, o], wy_p, wy_m, y_plus, y_minus
        )
        for o in (0, 1):
            w_y[o] = total(o).reshape(w_y.shape[1:])
        total = yield from ring_sum(
            x, X, lambda at, o: w_y.at[at // 2, at % 2, o], wx_p, wx_m, x_plus, x_minus
        )
        for o in (0, 1):
            w_z[z, o] = total(o)
        yield from ring_gather(z, Z, lambda at, o: w_z.at[at, o], z_plus, z_minus)
        full = w_z[0]
        for at in range(1, Z):
            full = full + w_z[at]
        w_x[k, y, x] = full
        yield from ring_gather(x, X, lambda at, o: w_x.at[k, y, at, o], x_plus, x_minus)
        yield from ring_gather(
            y, Y, lambda at, o: w_x.at[k, at, pl.ds(o * (X // 2), X // 2)], y_plus, y_minus
        )
        sem = fresh()
        send(w_x.at[k], w_x.at[k], sem, core_dev)
        yield
        arrived(w_x.at[1 - k], sem)

    weight_run = weight_steps()

    def weight_step(count):
        for _ in range(count):
            next(weight_run, None)

    gather_run = ring_gather(z, Z, gath_at, z_plus, z_minus, ready=gath_ready, on_block=to_core)
    next(gather_run)
    to_core(z, 1, 1, 0)
    weight_step(1)
    accumulate([(0, 1, 0), (1, 1, 0)], z, start=True)
    weight_step(1)
    for d in range(1, HZ + 1):
        next(gather_run, None)
        weight_step(2)
        if d < HZ:
            for s in (1, -1):
                accumulate([(0, s, d), (1, s, d)], (z - s * d + Z) % Z)
        else:
            accumulate([(0, 1, d), (1, -1, d)], (z + HZ) % Z)
        weight_step(2)

    back[...] = acc[...].astype(BF).reshape(back.shape)

    def back_at(at, o):
        return back.at[xh if o == 0 else 1 - xh, at]

    steps = ring_sum(y, Y, back_at, yp, ym, y_plus, y_minus)
    while True:
        try:
            next(steps)
            weight_step(1)
        except StopIteration as stop:
            total = stop.value
            break
    far_back = fresh()
    own_sum2 = yp.at[1, 1]
    own_sum2[...] = total(1).astype(BF)
    send(own_sum2, xb_in, far_back, x_far)
    mine = total(0)
    for _ in weight_run:
        pass
    weight_grad[...] = w_x[...].reshape(weight_grad.shape)
    arrived(xb_in, far_back)
    feat_grad[...] = (mine + xb_in[...].astype(F32)).astype(BF)
    for copy in pending:
        copy.wait_send()
    assert counters["send"] <= send_sems.shape[0] and counters["recv"] <= recv_sems.shape[0]


def local(n_row, n_col, feats, weight, cotangent, tile_values, tile_rows, tile_cols, tile_count):
    rows_here, width = feats.shape[1:]
    slots = tile_values.shape[2]
    Y, Z, X = n_row // X_HI, n_col // (X_LO * CORE), X_HI * X_LO
    row_tiles, col_tiles = n_col, n_row
    ids = tile_rows[0, 0] * col_tiles + tile_cols[0, 0]
    slot_ids = jnp.arange(slots, dtype=jnp.int32)
    ids = jnp.where(slot_ids < tile_count[0, 0], ids, -1)
    places = jnp.arange(row_tiles * col_tiles, dtype=jnp.int32)
    hit = ids[None, :] == places[:, None]
    tab = jnp.min(jnp.where(hit, slot_ids[None, :], slots), axis=1).reshape(row_tiles, col_tiles)

    block = (128, width)
    w_rows = width // (CORE * Y * X)
    scratch = [
        pltpu.VMEM((slots + 1, 128, 128), BF),
        pltpu.VMEM((row_tiles * 128, col_tiles * 128), BF),
        pltpu.VMEM((n_row,) + block, BF),
        pltpu.VMEM((Z, X_LO, CORE) + block, BF),
        pltpu.VMEM((Z, X_LO) + block, BF),
        pltpu.VMEM((Z // 2, 2) + block, BF),
        pltpu.VMEM((Z // 2, 2) + block, BF),
        pltpu.VMEM(block, BF),
        pltpu.VMEM(block, BF),
        pltpu.VMEM((Z, X_LO, CORE) + block, BF),
        pltpu.VMEM((col_tiles * 128, width), F32),
        pltpu.VMEM((X_HI, Y) + block, BF),
        pltpu.VMEM((Y // 2, 2) + block, BF),
        pltpu.VMEM((Y // 2, 2) + block, BF),
        pltpu.VMEM(block, BF),
        pltpu.VMEM((CORE, Y, 2, X * w_rows // 2, width), F32),
        pltpu.VMEM((Y, 2, X * w_rows // 2, width), F32),
        pltpu.VMEM((Y // 2, 2, X * w_rows // 2, width), F32),
        pltpu.VMEM((Y // 2, 2, X * w_rows // 2, width), F32),
        pltpu.VMEM((2, X // 2, 2, w_rows // 2, width), F32),
        pltpu.VMEM((X // 2, 2, w_rows // 2, width), F32),
        pltpu.VMEM((X // 2, 2, w_rows // 2, width), F32),
        pltpu.VMEM((CORE, Y, X, 2, w_rows // 2, width), F32),
        pltpu.VMEM((Z, 2, w_rows // 2, width), F32),
        pltpu.SemaphoreType.DMA,
        pltpu.SemaphoreType.DMA((140,)),
        pltpu.SemaphoreType.DMA((170,)),
        pltpu.SemaphoreType.DMA((Z,)),
        pltpu.SemaphoreType.DMA((Z,)),
    ]
    vmem = pl.BlockSpec(memory_space=pltpu.VMEM)
    layer_out, feat_grad, weight_grad = pl.pallas_call(
        functools.partial(layer_kernel, n_row, n_col),
        out_shape=(
            jax.ShapeDtypeStruct(block, BF),
            jax.ShapeDtypeStruct(block, BF),
            jax.ShapeDtypeStruct((width, width), F32),
        ),
        in_specs=[
            pl.BlockSpec(memory_space=pltpu.SMEM), vmem, vmem, vmem,
            pl.BlockSpec(memory_space=pl.ANY),
        ],
        out_specs=(vmem, vmem, vmem),
        scratch_shapes=scratch,
        compiler_params=pltpu.CompilerParams(
            collective_id=0, has_side_effects=True, vmem_limit_bytes=60 * 1024 * 1024
        ),
    )(tab, feats[0], weight, cotangent[0], tile_values[0, 0])
    return layer_out[None], feat_grad[None], weight_grad


def solution(mesh):
    in_specs = (
        P("col", "row", None),
        P(),
        P("row", "col", None),
        P("row", "col", None, None, None),
        P("row", "col", None),
        P("row", "col", None),
        P("row", "col"),
    )
    out_specs = (P("row", "col", None), P("col", "row", None), P())
    return jax.shard_map(
        functools.partial(local, mesh.shape["row"], mesh.shape["col"]),
        mesh=mesh, in_specs=in_specs, out_specs=out_specs, check_vma=False,
    )
```

```python
import functools

import jax
import jax.numpy as jnp
from jax import lax
from jax.experimental import pallas as pl
from jax.experimental.pallas import tpu as pltpu
from jax.sharding import PartitionSpec as P

BF = jnp.bfloat16
F32 = jnp.float32
X_HI, X_LO, CORE = 2, 2, 2


def layer_kernel(
    n_row, n_col, tab, feats_hbm, weight_hbm, cot_hbm, tiles_hbm, layer_hbm, feat_grad_hbm, weight_grad_hbm,
    weight, cot, layer_out, feat_grad, tiles, dense, panel, part, core_in, rp, rm, own_sum, x_in, gath, acc, back, yp, ym, xb_in,
    w_term, w_core, wy_p, wy_m, w_y, wx_p, wx_m, w_x, w_z,
    tile_sem, local_sems, send_sems, recv_sems, core_send, core_recv,
):
    Y, Z = n_row // X_HI, n_col // (X_LO * CORE)
    X = X_HI * X_LO
    HZ = Z // 2
    slots = tiles_hbm.shape[2]
    row_tiles, col_tiles = n_col, n_row
    chunk = row_tiles * 128 // Z
    width = feats_hbm.shape[2]
    half_rows = 64

    r, c = lax.axis_index("row"), lax.axis_index("col")
    xh, y = r // Y, r % Y
    z, xl, k = c // (X_LO * CORE), (c // CORE) % X_LO, c % CORE
    x = xh * X_LO + xl

    def device(x_at, y_at, z_at, k_at):
        return ((x_at // X_LO) * Y + y_at, z_at * (X_LO * CORE) + (x_at % X_LO) * CORE + k_at)

    core_dev = device(x, y, z, 1 - k)
    x_plus, x_minus = device((x + 1) % X, y, z, k), device((x + X - 1) % X, y, z, k)
    x_far = device((x + 2) % X, y, z, k)
    x_near = device(xh * X_LO + 1 - xl, y, z, k)
    y_plus, y_minus = device(x, (y + 1) % Y, z, k), device(x, (y + Y - 1) % Y, z, k)
    z_plus, z_minus = device(x, y, (z + 1) % Z, k), device(x, y, (z + Z - 1) % Z, k)

    pending = []
    counters = {"send": 0, "recv": 0}

    def fresh():
        counters["recv"] += 1
        return counters["recv"] - 1

    def remote(src, dst, sem_out, sem_in, dev):
        return pltpu.make_async_remote_copy(
            src_ref=src, dst_ref=dst, send_sem=sem_out, recv_sem=sem_in,
            device_id=dev, device_id_type=pl.DeviceIdType.MESH,
        )

    def send(src, dst, sem, dev):
        copy = remote(src, dst, send_sems.at[counters["send"]], recv_sems.at[sem], dev)
        counters["send"] += 1
        copy.start()
        pending.append(copy)

    def arrived(view, sem):
        remote(view, view, send_sems.at[0], recv_sems.at[sem], core_dev).wait_recv()

    def add_into(dst, other):
        dst[...] = (dst[...].astype(F32) + other[...].astype(F32)).astype(dst.dtype)

    def ring_gather(pos, n, view, plus, minus, ready=None, on_block=None):
        half = n // 2
        sems = {(s, d, o): fresh() for s in (1, -1) for d in range(1, half + 1) for o in (0, 1)}

        def goes(s, d, o):
            return d < half or (d == half and o == (0 if s == 1 else 1))

        for o in (0, 1):
            if ready is not None:
                ready(o)
            for s in (1, -1):
                if goes(s, 1, o):
                    send(view(pos, o), view(pos, o), sems[s, 1, o], plus if s == 1 else minus)
        for d in range(1, half + 1):
            yield
            for o in (0, 1):
                for s in (1, -1):
                    if not goes(s, d, o):
                        continue
                    at = (pos - s * d + n) % n
                    arrived(view(at, o), sems[s, d, o])
                    if goes(s, d + 1, o):
                        send(view(at, o), view(at, o), sems[s, d + 1, o], plus if s == 1 else minus)
                    if on_block is not None:
                        on_block(at, o, s, d)

    def ring_sum(pos, n, view, bufs_p, bufs_m, plus, minus, before=None):
        half = n // 2
        bufs, dev = {1: bufs_p, -1: bufs_m}, {1: plus, -1: minus}
        sems = {(s, d, o): fresh() for s in (1, -1) for d in range(half) for o in (0, 1)}
        first = {(1, 0): half, (1, 1): half - 1, (-1, 1): half, (-1, 0): half - 1}
        for o in (0, 1):
            for s in (1, -1):
                d = first[s, o]
                if d > 0 and d == half:
                    send(view((pos + s * d + n) % n, o), bufs[s].at[d - 1, o], sems[s, d - 1, o], dev[s])
        for o in (1, 0):
            for s in (1, -1):
                d = first[s, o]
                if d > 0 and d < half:
                    send(view((pos + s * d + n) % n, o), bufs[s].at[d - 1, o], sems[s, d - 1, o], dev[s])
        for d in range(half - 1, 0, -1):
            yield
            if before is not None:
                before(d)
            for o in (1, 0):
                for s in (1, -1):
                    if d >= first[s, o]:
                        continue
                    buf = bufs[s].at[d, o]
                    arrived(buf, sems[s, d, o])
                    add_into(buf, view((pos + s * d + n) % n, o))
                    send(buf, bufs[s].at[d - 1, o], sems[s, d - 1, o], dev[s])
        yield
        if before is not None:
            before(0)

        def total(o):
            value = view(pos, o)[...].astype(F32)
            for s in (1, -1):
                if first[s, o] > 0:
                    arrived(bufs[s].at[0, o], sems[s, 0, o])
                    value = value + bufs[s][0, o].astype(F32)
            return value

        return total

    def panel_at(at, o):
        return panel.at[(xh if o == 0 else 1 - xh) * Y + at]

    feats_copy = pltpu.make_async_copy(feats_hbm.at[0], panel_at(y, 0), local_sems.at[0])
    feats_copy.start()
    weight_copy = pltpu.make_async_copy(weight_hbm, weight, local_sems.at[1])
    cot_copy = pltpu.make_async_copy(cot_hbm.at[0], cot, local_sems.at[2])
    tile_copy = pltpu.make_async_copy(tiles_hbm.at[0, 0], tiles.at[pl.ds(0, slots)], tile_sem)
    tile_copy.start()
    barrier = pltpu.get_barrier_semaphore()
    peers = (core_dev, x_plus, x_minus, x_far, y_plus, y_minus, z_plus, z_minus)
    for dev in peers:
        pl.semaphore_signal(barrier, inc=1, device_id=dev, device_id_type=pl.DeviceIdType.MESH)
    weight_copy.start()
    cot_copy.start()
    tiles[slots] = jnp.zeros(tiles.shape[1:], tiles.dtype)
    feats_copy.wait()
    pl.semaphore_wait(barrier, len(peers))

    far_sem = fresh()
    send(panel_at(y, 0), panel_at(y, 0), far_sem, x_far)

    def densify():
        tile_copy.wait()

        def one_row(i, carry):
            for j in range(col_tiles):
                dense[pl.ds(pl.multiple_of(i * 128, 128), 128), j * 128 : (j + 1) * 128] = tiles[tab[i * col_tiles + j]]
            return carry

        lax.fori_loop(0, row_tiles, one_row, 0)

    def panel_ready(o):
        if o == 1:
            densify()
            arrived(panel_at(y, 1), far_sem)

    for _ in ring_gather(y, Y, panel_at, y_plus, y_minus, ready=panel_ready):
        pass

    def forward_chunk(t, carry):
        off = HZ + (1 - 2 * (t % 2)) * ((t + 1) // 2)
        at = (z + off) % Z
        product = jnp.dot(
            dense[pl.ds(pl.multiple_of(at * chunk, chunk), chunk), :],
            panel[...].reshape(col_tiles * 128, width),
            preferred_element_type=F32,
        )
        part[at] = product.astype(BF).reshape(X_LO, CORE, 128, width)
        remote(
            part.at[at, :, 1 - k], core_in.at[at], core_send.at[t], core_recv.at[t], core_dev
        ).start()
        return carry

    def core_total(t):
        off = HZ + (1 - 2 * (t % 2)) * ((t + 1) // 2)
        at = (z + off) % Z
        remote(
            part.at[at, :, 1 - k], core_in.at[at], core_send.at[t], core_recv.at[t], core_dev
        ).wait()
        for o in range(X_LO):
            add_into(core_in.at[at, o], part.at[at, o, k])

    def sum_at(at, o):
        return core_in.at[at, xl if o == 0 else 1 - xl]

    lax.fori_loop(0, 3, forward_chunk, 0)
    for t in range(3):
        core_total(t)

    done = [3]

    def before(d):
        if d == HZ - 1:
            lax.fori_loop(3, Z, forward_chunk, 0)
        while done[0] < Z and d <= HZ - 2 and done[0] <= 2 * (HZ - d):
            core_total(done[0])
            done[0] += 1

    steps = ring_sum(z, Z, sum_at, rp, rm, z_plus, z_minus, before=before)
    while True:
        try:
            next(steps)
        except StopIteration as stop:
            total = stop.value
            break
    x_sem = fresh()
    own_sum[...] = total(1).astype(BF)
    send(own_sum, x_in, x_sem, x_near)
    mine = total(0)
    arrived(x_in, x_sem)
    summed = (mine + x_in[...].astype(F32)).astype(BF)

    weight_copy.wait()
    cot_copy.wait()
    hidden = jnp.dot(summed, weight[...], preferred_element_type=F32)
    gate = jax.nn.sigmoid(hidden)
    hidden_grad = (cot[...].astype(F32) * gate * (1.0 + hidden * (1.0 - gate))).astype(BF)
    grad_rows = lax.dot_general(
        hidden_grad, weight[...], (((1,), (1,)), ((), ())), preferred_element_type=F32
    ).astype(BF)
    gath[z, xl, k] = grad_rows

    def piece(at, p, core):
        slot = xl if p == 0 else 1 - xl
        if p == 0:
            return gath.at[at, slot, core]
        return gath.at[at, slot, core, pl.ds((p - 1) * half_rows, half_rows)]

    def own_half(at, h):
        return gath.at[at, xl, k, pl.ds(h * half_rows, half_rows)]

    pair_sems, near_sems = {}, {}

    def to_core(at, p, s, d):
        pair_sems[p, s, d] = fresh()
        send(piece(at, p, k), piece(at, p, k), pair_sems[p, s, d], core_dev)

    def to_near(at, h, s, d):
        near_sems[h, s, d] = fresh()
        send(own_half(at, h), own_half(at, h), near_sems[h, s, d], x_near)

    def from_near(at, h, s, d):
        arrived(piece(at, 1 + h, k), near_sems[h, s, d])

    to_near(z, 0, 1, 0)
    layer_copy = pltpu.make_async_copy(layer_out, layer_hbm.at[0], local_sems.at[3])

    def gath_ready(o):
        if o == 1:
            to_near(z, 1, 1, 0)
            to_core(z, 0, 1, 0)
            layer_out[...] = (hidden * gate).astype(BF)
            layer_copy.start()
            w_term[...] = (
                lax.dot_general(summed, hidden_grad, (((0,), (0,)), ((), ())), preferred_element_type=F32)
                * (n_row * n_col * 128) ** (-0.5)
            ).reshape(w_term.shape)
            from_near(z, 0, 1, 0)

    def gath_block(at, o, s, d):
        if o == 0 and d < HZ:
            to_near(at, 1, s, d)
        to_core(at, o, s, d)

    last_sem = fresh()

    def backward_chunk(at):
        product = lax.dot_general(
            dense[pl.ds(pl.multiple_of(at * chunk, chunk), chunk), :],
            gath[at].reshape(chunk, width),
            (((0,), (0,)), ((), ())),
            preferred_element_type=F32,
        )
        return product

    def accumulate(keys, at, start=False):
        for p, s, d in keys:
            arrived(piece(at, p, 1 - k), pair_sems[p, s, d])
        if start:
            acc[...] = backward_chunk(at)
        else:
            acc[...] += backward_chunk(at)

    def weight_steps():
        sem = fresh()
        send(w_term.at[1 - k], w_core, sem, core_dev)
        yield
        arrived(w_core, sem)
        add_into(w_core, w_term.at[k])
        total = yield from ring_sum(
            y, Y, lambda at, o: w_core.at[at, o], wy_p, wy_m, y_plus, y_minus
        )
        for o in (0, 1):
            w_y[o] = total(o).reshape(w_y.shape[1:])
        total = yield from ring_sum(
            x, X, lambda at, o: w_y.at[at // 2, at % 2, o], wx_p, wx_m, x_plus, x_minus
        )
        for o in (0, 1):
            w_z[z, o] = total(o)
        yield from ring_gather(z, Z, lambda at, o: w_z.at[at, o], z_plus, z_minus)
        full = w_z[0]
        for at in range(1, Z):
            full = full + w_z[at]
        w_x[k, y, x] = full
        yield from ring_gather(x, X, lambda at, o: w_x.at[k, y, at, o], x_plus, x_minus)
        yield from ring_gather(
            y, Y, lambda at, o: w_x.at[k, at, pl.ds(o * (X // 2), X // 2)], y_plus, y_minus
        )
        sem = fresh()
        send(w_x.at[k], w_x.at[k], sem, core_dev)
        yield
        arrived(w_x.at[1 - k], sem)

    weight_run = weight_steps()

    def weight_step(count):
        for _ in range(count):
            next(weight_run, None)

    gather_run = ring_gather(
        z, Z, lambda at, o: piece(at, o, k), z_plus, z_minus, ready=gath_ready, on_block=gath_block
    )
    next(gather_run)
    to_core(z, 1, 1, 0)
    weight_step(1)
    from_near(z, 1, 1, 0)
    to_core(z, 2, 1, 0)
    weight_step(1)
    for d in range(1, HZ + 1):
        next(gather_run, None)
        weight_step(2)
        if d == 1:
            accumulate([(p, 1, 0) for p in range(3)], z, start=True)
        else:
            for s in (1, -1):
                accumulate([(p, s, d - 1) for p in range(3)], (z - s * (d - 1) + Z) % Z)
        weight_step(2)
        if d < HZ:
            for s in (-1, 1):
                at = (z - s * d + Z) % Z
                from_near(at, 1, s, d)
                if d == HZ - 1 and s == -1:
                    send(piece(at, 2, k), piece(at, 2, k), last_sem, z_minus)
                to_core(at, 2, s, d)
    far = (z + HZ) % Z
    arrived(piece(far, 2, k), last_sem)
    to_core(far, 2, -1, HZ)
    accumulate([(0, 1, HZ), (1, -1, HZ), (2, -1, HZ)], far)

    back[...] = acc[...].astype(BF).reshape(back.shape)

    def back_at(at, o):
        return back.at[xh if o == 0 else 1 - xh, at]

    steps = ring_sum(y, Y, back_at, yp, ym, y_plus, y_minus)
    while True:
        try:
            next(steps)
            weight_step(1)
        except StopIteration as stop:
            total = stop.value
            break
    far_back = fresh()
    own_sum2 = yp.at[1, 1]
    own_sum2[...] = total(1).astype(BF)
    send(own_sum2, xb_in, far_back, x_far)
    mine = total(0)
    for _ in weight_run:
        pass
    weight_grad_copy = pltpu.make_async_copy(w_x, weight_grad_hbm.reshape(w_x.shape), local_sems.at[4])
    weight_grad_copy.start()
    arrived(xb_in, far_back)
    feat_grad[...] = (mine + xb_in[...].astype(F32)).astype(BF)
    feat_grad_copy = pltpu.make_async_copy(feat_grad, feat_grad_hbm.at[0], local_sems.at[5])
    feat_grad_copy.start()
    for copy in pending:
        copy.wait_send()
    layer_copy.wait()
    weight_grad_copy.wait()
    feat_grad_copy.wait()
    assert counters["send"] <= send_sems.shape[0] and counters["recv"] <= recv_sems.shape[0]


def write_outputs(layer_out, feat_grad, weight_grad, layer_hbm, feat_grad_hbm, weight_grad_hbm, sems):
    pairs = ((weight_grad, weight_grad_hbm), (feat_grad, feat_grad_hbm), (layer_out, layer_hbm))
    copies = [pltpu.make_async_copy(src, dst, sems.at[i]) for i, (src, dst) in enumerate(pairs)]
    for copy in copies:
        copy.start()
    for copy in copies:
        copy.wait()


def local(n_row, n_col, feats, weight, cotangent, tile_values, tile_rows, tile_cols, tile_count):
    rows_here, width = feats.shape[1:]
    slots = tile_values.shape[2]
    Y, Z, X = n_row // X_HI, n_col // (X_LO * CORE), X_HI * X_LO
    row_tiles, col_tiles = n_col, n_row
    ids = tile_rows[0, 0] * col_tiles + tile_cols[0, 0]
    slot_ids = jnp.arange(slots, dtype=jnp.int32)
    ids = jnp.where(slot_ids < tile_count[0, 0], ids, -1)
    places = jnp.arange(row_tiles * col_tiles, dtype=jnp.int32)
    hit = ids[None, :] == places[:, None]
    tab = jnp.min(jnp.where(hit, slot_ids[None, :], slots), axis=1)

    block = (128, width)
    w_rows = width // (CORE * Y * X)
    w_full = (CORE, Y, X, 2, w_rows // 2, width)
    scratch = [
        pltpu.VMEM((width, width), BF),
        pltpu.VMEM(block, BF),
        pltpu.VMEM(block, BF),
        pltpu.VMEM(block, BF),
        pltpu.VMEM((slots + 1, 128, 128), BF),
        pltpu.VMEM((row_tiles * 128, col_tiles * 128), BF),
        pltpu.VMEM((n_row,) + block, BF),
        pltpu.VMEM((Z, X_LO, CORE) + block, BF),
        pltpu.VMEM((Z, X_LO) + block, BF),
        pltpu.VMEM((Z // 2, 2) + block, BF),
        pltpu.VMEM((Z // 2, 2) + block, BF),
        pltpu.VMEM(block, BF),
        pltpu.VMEM(block, BF),
        pltpu.VMEM((Z, X_LO, CORE) + block, BF),
        pltpu.VMEM((col_tiles * 128, width), F32),
        pltpu.VMEM((X_HI, Y) + block, BF),
        pltpu.VMEM((Y // 2, 2) + block, BF),
        pltpu.VMEM((Y // 2, 2) + block, BF),
        pltpu.VMEM(block, BF),
        pltpu.VMEM((CORE, Y, 2, X * w_rows // 2, width), F32),
        pltpu.VMEM((Y, 2, X * w_rows // 2, width), F32),
        pltpu.VMEM((Y // 2, 2, X * w_rows // 2, width), F32),
        pltpu.VMEM((Y // 2, 2, X * w_rows // 2, width), F32),
        pltpu.VMEM((2, X // 2, 2, w_rows // 2, width), F32),
        pltpu.VMEM((X // 2, 2, w_rows // 2, width), F32),
        pltpu.VMEM((X // 2, 2, w_rows // 2, width), F32),
        pltpu.VMEM(w_full, F32),
        pltpu.VMEM((Z, 2, w_rows // 2, width), F32),
        pltpu.SemaphoreType.DMA,
        pltpu.SemaphoreType.DMA((6,)),
        pltpu.SemaphoreType.DMA((180,)),
        pltpu.SemaphoreType.DMA((210,)),
        pltpu.SemaphoreType.DMA((Z,)),
        pltpu.SemaphoreType.DMA((Z,)),
    ]
    hbm = pl.BlockSpec(memory_space=pltpu.HBM)
    layer_out, feat_grad, weight_grad = pl.pallas_call(
        functools.partial(layer_kernel, n_row, n_col),
        out_shape=(
            jax.ShapeDtypeStruct((1,) + block, BF),
            jax.ShapeDtypeStruct((1,) + block, BF),
            jax.ShapeDtypeStruct((width, width), F32),
        ),
        in_specs=[pl.BlockSpec(memory_space=pltpu.SMEM), hbm, hbm, hbm, hbm],
        out_specs=(hbm, hbm, hbm),
        scratch_shapes=scratch,
        compiler_params=pltpu.CompilerParams(
            collective_id=0, has_side_effects=True, vmem_limit_bytes=60 * 1024 * 1024
        ),
    )(tab, feats, weight, cotangent, tile_values)
    return pl.pallas_call(
        write_outputs,
        out_shape=(
            jax.ShapeDtypeStruct((1,) + block, BF),
            jax.ShapeDtypeStruct((1,) + block, BF),
            jax.ShapeDtypeStruct((width, width), F32),
        ),
        in_specs=[hbm, hbm, hbm],
        out_specs=(hbm, hbm, hbm),
        scratch_shapes=[pltpu.SemaphoreType.DMA((3,))],
    )(layer_out, feat_grad, weight_grad)


def solution(mesh):
    in_specs = (
        P("col", "row", None),
        P(),
        P("row", "col", None),
        P("row", "col", None, None, None),
        P("row", "col", None),
        P("row", "col", None),
        P("row", "col"),
    )
    out_specs = (P("row", "col", None), P("col", "row", None), P())
    return jax.shard_map(
        functools.partial(local, mesh.shape["row"], mesh.shape["col"]),
        mesh=mesh, in_specs=in_specs, out_specs=out_specs, check_vma=False,
    )
```

```python
import functools

import jax
import jax.numpy as jnp
from jax import lax
from jax.experimental import pallas as pl
from jax.experimental.pallas import tpu as pltpu
from jax.sharding import PartitionSpec as P

BF = jnp.bfloat16
F32 = jnp.float32
X_HI, X_LO, CORE = 2, 2, 2


def layer_kernel(
    n_row, n_col, tab, feats_hbm, weight_hbm, cot_hbm, tiles_hbm, layer_hbm, feat_grad_hbm, weight_grad_hbm,
    weight, cot, layer_out, feat_grad, tiles, dense, panel, part, core_in, rp, rm, own_sum, x_in, gath, acc, back, yp, ym, xb_in,
    w_term, w_core, wy_p, wy_m, w_y, wx_p, wx_m, w_x, w_z,
    tile_sem, local_sems, send_sems, recv_sems, core_send, core_recv,
):
    Y, Z = n_row // X_HI, n_col // (X_LO * CORE)
    X = X_HI * X_LO
    HZ = Z // 2
    slots = tiles_hbm.shape[2]
    row_tiles, col_tiles = n_col, n_row
    chunk = row_tiles * 128 // Z
    width = feats_hbm.shape[2]
    half_rows = 64

    r, c = lax.axis_index("row"), lax.axis_index("col")
    xh, y = r // Y, r % Y
    z, xl, k = c // (X_LO * CORE), (c // CORE) % X_LO, c % CORE
    x = xh * X_LO + xl

    def device(x_at, y_at, z_at, k_at):
        return ((x_at // X_LO) * Y + y_at, z_at * (X_LO * CORE) + (x_at % X_LO) * CORE + k_at)

    core_dev = device(x, y, z, 1 - k)
    x_plus, x_minus = device((x + 1) % X, y, z, k), device((x + X - 1) % X, y, z, k)
    x_far = device((x + 2) % X, y, z, k)
    x_near = device(xh * X_LO + 1 - xl, y, z, k)
    y_plus, y_minus = device(x, (y + 1) % Y, z, k), device(x, (y + Y - 1) % Y, z, k)
    z_plus, z_minus = device(x, y, (z + 1) % Z, k), device(x, y, (z + Z - 1) % Z, k)

    pending = []
    counters = {"send": 0, "recv": 0}

    def fresh():
        counters["recv"] += 1
        return counters["recv"] - 1

    def remote(src, dst, sem_out, sem_in, dev):
        return pltpu.make_async_remote_copy(
            src_ref=src, dst_ref=dst, send_sem=sem_out, recv_sem=sem_in,
            device_id=dev, device_id_type=pl.DeviceIdType.MESH,
        )

    def send(src, dst, sem, dev):
        copy = remote(src, dst, send_sems.at[counters["send"]], recv_sems.at[sem], dev)
        counters["send"] += 1
        copy.start()
        pending.append(copy)

    def arrived(view, sem):
        remote(view, view, send_sems.at[0], recv_sems.at[sem], core_dev).wait_recv()

    def add_into(dst, other):
        dst[...] = (dst[...].astype(F32) + other[...].astype(F32)).astype(dst.dtype)

    def ring_gather(pos, n, view, plus, minus, ready=None, on_block=None):
        half = n // 2
        sems = {(s, d, o): fresh() for s in (1, -1) for d in range(1, half + 1) for o in (0, 1)}

        def goes(s, d, o):
            return d < half or (d == half and o == (0 if s == 1 else 1))

        for o in (0, 1):
            if ready is not None:
                ready(o)
            for s in (1, -1):
                if goes(s, 1, o):
                    send(view(pos, o), view(pos, o), sems[s, 1, o], plus if s == 1 else minus)
        for d in range(1, half + 1):
            yield
            for o in (0, 1):
                for s in (1, -1):
                    if not goes(s, d, o):
                        continue
                    at = (pos - s * d + n) % n
                    arrived(view(at, o), sems[s, d, o])
                    if goes(s, d + 1, o):
                        send(view(at, o), view(at, o), sems[s, d + 1, o], plus if s == 1 else minus)
                    if on_block is not None:
                        on_block(at, o, s, d)

    def ring_sum(pos, n, view, bufs_p, bufs_m, plus, minus, before=None):
        half = n // 2
        bufs, dev = {1: bufs_p, -1: bufs_m}, {1: plus, -1: minus}
        sems = {(s, d, o): fresh() for s in (1, -1) for d in range(half) for o in (0, 1)}
        first = {(1, 0): half, (1, 1): half - 1, (-1, 1): half, (-1, 0): half - 1}
        for o in (0, 1):
            for s in (1, -1):
                d = first[s, o]
                if d > 0 and d == half:
                    send(view((pos + s * d + n) % n, o), bufs[s].at[d - 1, o], sems[s, d - 1, o], dev[s])
        for o in (1, 0):
            for s in (1, -1):
                d = first[s, o]
                if d > 0 and d < half:
                    send(view((pos + s * d + n) % n, o), bufs[s].at[d - 1, o], sems[s, d - 1, o], dev[s])
        for d in range(half - 1, 0, -1):
            yield
            if before is not None:
                before(d)
            for o in (1, 0):
                for s in (1, -1):
                    if d >= first[s, o]:
                        continue
                    buf = bufs[s].at[d, o]
                    arrived(buf, sems[s, d, o])
                    add_into(buf, view((pos + s * d + n) % n, o))
                    send(buf, bufs[s].at[d - 1, o], sems[s, d - 1, o], dev[s])
        yield
        if before is not None:
            before(0)

        def total(o):
            value = view(pos, o)[...].astype(F32)
            for s in (1, -1):
                if first[s, o] > 0:
                    arrived(bufs[s].at[0, o], sems[s, 0, o])
                    value = value + bufs[s][0, o].astype(F32)
            return value

        return total

    def panel_at(at, o):
        return panel.at[(xh if o == 0 else 1 - xh) * Y + at]

    feats_copy = pltpu.make_async_copy(feats_hbm.at[0], panel_at(y, 0), local_sems.at[0])
    feats_copy.start()
    weight_copy = pltpu.make_async_copy(weight_hbm, weight, local_sems.at[1])
    cot_copy = pltpu.make_async_copy(cot_hbm.at[0], cot, local_sems.at[2])
    tile_copy = pltpu.make_async_copy(tiles_hbm.at[0, 0], tiles.at[pl.ds(0, slots)], tile_sem)
    tile_copy.start()
    barrier = pltpu.get_barrier_semaphore()
    peers = (core_dev, x_plus, x_minus, x_far, y_plus, y_minus, z_plus, z_minus)
    for dev in peers:
        pl.semaphore_signal(barrier, inc=1, device_id=dev, device_id_type=pl.DeviceIdType.MESH)
    weight_copy.start()
    cot_copy.start()
    tiles[slots] = jnp.zeros(tiles.shape[1:], tiles.dtype)
    feats_copy.wait()
    pl.semaphore_wait(barrier, len(peers))

    far_sem = fresh()
    send(panel_at(y, 0), panel_at(y, 0), far_sem, x_far)

    def densify():
        tile_copy.wait()

        def one_row(i, carry):
            for j in range(col_tiles):
                dense[pl.ds(pl.multiple_of(i * 128, 128), 128), j * 128 : (j + 1) * 128] = tiles[tab[i * col_tiles + j]]
            return carry

        lax.fori_loop(0, row_tiles, one_row, 0)

    def panel_ready(o):
        if o == 1:
            densify()
            arrived(panel_at(y, 1), far_sem)

    for _ in ring_gather(y, Y, panel_at, y_plus, y_minus, ready=panel_ready):
        pass

    def forward_chunk(t, carry):
        off = HZ + (1 - 2 * (t % 2)) * ((t + 1) // 2)
        at = (z + off) % Z
        product = jnp.dot(
            dense[pl.ds(pl.multiple_of(at * chunk, chunk), chunk), :],
            panel[...].reshape(col_tiles * 128, width),
            preferred_element_type=F32,
        )
        part[at] = product.astype(BF).reshape(X_LO, CORE, 128, width)
        remote(
            part.at[at, :, 1 - k], core_in.at[at], core_send.at[t], core_recv.at[t], core_dev
        ).start()
        return carry

    def core_total(t):
        off = HZ + (1 - 2 * (t % 2)) * ((t + 1) // 2)
        at = (z + off) % Z
        remote(
            part.at[at, :, 1 - k], core_in.at[at], core_send.at[t], core_recv.at[t], core_dev
        ).wait()
        for o in range(X_LO):
            add_into(core_in.at[at, o], part.at[at, o, k])

    def sum_at(at, o):
        return core_in.at[at, xl if o == 0 else 1 - xl]

    lax.fori_loop(0, 3, forward_chunk, 0)
    for t in range(3):
        core_total(t)

    done = [3]

    def before(d):
        if d == HZ - 1:
            lax.fori_loop(3, Z, forward_chunk, 0)
        while done[0] < Z and d <= HZ - 2 and done[0] <= 2 * (HZ - d):
            core_total(done[0])
            done[0] += 1

    steps = ring_sum(z, Z, sum_at, rp, rm, z_plus, z_minus, before=before)
    while True:
        try:
            next(steps)
        except StopIteration as stop:
            total = stop.value
            break
    x_sem = fresh()
    own_sum[...] = total(1).astype(BF)
    send(own_sum, x_in, x_sem, x_near)
    mine = total(0)
    arrived(x_in, x_sem)
    summed = (mine + x_in[...].astype(F32)).astype(BF)

    weight_copy.wait()
    cot_copy.wait()
    hidden = jnp.dot(summed, weight[...], preferred_element_type=F32)
    gate = jax.nn.sigmoid(hidden)
    hidden_grad = (cot[...].astype(F32) * gate * (1.0 + hidden * (1.0 - gate))).astype(BF)
    grad_rows = lax.dot_general(
        hidden_grad, weight[...], (((1,), (1,)), ((), ())), preferred_element_type=F32
    ).astype(BF)
    gath[z, xl, k] = grad_rows

    def piece(at, p, core):
        slot = xl if p == 0 else 1 - xl
        if p == 0:
            return gath.at[at, slot, core]
        return gath.at[at, slot, core, pl.ds((p - 1) * half_rows, half_rows)]

    def own_half(at, h):
        return gath.at[at, xl, k, pl.ds(h * half_rows, half_rows)]

    pair_sems, near_sems = {}, {}

    def to_core(at, p, s, d):
        pair_sems[p, s, d] = fresh()
        send(piece(at, p, k), piece(at, p, k), pair_sems[p, s, d], core_dev)

    def to_near(at, h, s, d):
        near_sems[h, s, d] = fresh()
        send(own_half(at, h), own_half(at, h), near_sems[h, s, d], x_near)

    def from_near(at, h, s, d):
        arrived(piece(at, 1 + h, k), near_sems[h, s, d])

    to_near(z, 0, 1, 0)
    layer_copy = pltpu.make_async_copy(layer_out, layer_hbm.at[0], local_sems.at[3])

    def gath_ready(o):
        if o == 1:
            to_near(z, 1, 1, 0)
            to_core(z, 0, 1, 0)
            layer_out[...] = (hidden * gate).astype(BF)
            layer_copy.start()
            w_term[...] = (
                lax.dot_general(summed, hidden_grad, (((0,), (0,)), ((), ())), preferred_element_type=F32)
                * (n_row * n_col * 128) ** (-0.5)
            ).reshape(w_term.shape)
            from_near(z, 0, 1, 0)

    def gath_block(at, o, s, d):
        if o == 0 and d < HZ:
            to_near(at, 1, s, d)
        to_core(at, o, s, d)

    last_sem = fresh()

    def backward_chunk(at):
        product = lax.dot_general(
            dense[pl.ds(pl.multiple_of(at * chunk, chunk), chunk), :],
            gath[at].reshape(chunk, width),
            (((0,), (0,)), ((), ())),
            preferred_element_type=F32,
        )
        return product

    def accumulate(keys, at, start=False):
        for p, s, d in keys:
            arrived(piece(at, p, 1 - k), pair_sems[p, s, d])
        if start:
            acc[...] = backward_chunk(at)
        else:
            acc[...] += backward_chunk(at)

    def weight_steps():
        sem = fresh()
        send(w_term.at[1 - k], w_core, sem, core_dev)
        yield
        arrived(w_core, sem)
        add_into(w_core, w_term.at[k])
        total = yield from ring_sum(
            y, Y, lambda at, o: w_core.at[at, o], wy_p, wy_m, y_plus, y_minus
        )
        for o in (0, 1):
            w_y[o] = total(o).reshape(w_y.shape[1:])
        total = yield from ring_sum(
            x, X, lambda at, o: w_y.at[at // 2, at % 2, o], wx_p, wx_m, x_plus, x_minus
        )
        for o in (0, 1):
            w_z[z, o] = total(o)
        yield from ring_gather(z, Z, lambda at, o: w_z.at[at, o], z_plus, z_minus)
        full = w_z[0]
        for at in range(1, Z):
            full = full + w_z[at]
        w_x[k, y, x] = full
        yield from ring_gather(x, X, lambda at, o: w_x.at[k, y, at, o], x_plus, x_minus)
        yield from ring_gather(
            y, Y, lambda at, o: w_x.at[k, at, pl.ds(o * (X // 2), X // 2)], y_plus, y_minus
        )
        sem = fresh()
        send(w_x.at[k], w_x.at[k], sem, core_dev)
        yield
        arrived(w_x.at[1 - k], sem)

    weight_run = weight_steps()

    def weight_step(count):
        for _ in range(count):
            next(weight_run, None)

    gather_run = ring_gather(
        z, Z, lambda at, o: piece(at, o, k), z_plus, z_minus, ready=gath_ready, on_block=gath_block
    )
    next(gather_run)
    to_core(z, 1, 1, 0)
    weight_step(1)
    from_near(z, 1, 1, 0)
    to_core(z, 2, 1, 0)
    weight_step(1)
    for d in range(1, HZ + 1):
        next(gather_run, None)
        weight_step(1)
        if d == 1:
            accumulate([(p, 1, 0) for p in range(3)], z, start=True)
        else:
            for s in (1, -1):
                accumulate([(p, s, d - 1) for p in range(3)], (z - s * (d - 1) + Z) % Z)
        weight_step(1)
        if d < HZ:
            for s in (-1, 1):
                at = (z - s * d + Z) % Z
                from_near(at, 1, s, d)
                if d == HZ - 1 and s == -1:
                    send(piece(at, 2, k), piece(at, 2, k), last_sem, z_minus)
                to_core(at, 2, s, d)
    far = (z + HZ) % Z
    arrived(piece(far, 2, k), last_sem)
    to_core(far, 2, -1, HZ)
    accumulate([(0, 1, HZ), (1, -1, HZ), (2, -1, HZ)], far)

    back[...] = acc[...].astype(BF).reshape(back.shape)

    def back_at(at, o):
        return back.at[xh if o == 0 else 1 - xh, at]

    steps = ring_sum(y, Y, back_at, yp, ym, y_plus, y_minus)
    while True:
        try:
            next(steps)
            weight_step(1)
        except StopIteration as stop:
            total = stop.value
            break
    far_back = fresh()
    own_sum2 = yp.at[1, 1]
    own_sum2[...] = total(1).astype(BF)
    send(own_sum2, xb_in, far_back, x_far)
    mine = total(0)
    for _ in weight_run:
        pass
    weight_grad_copy = pltpu.make_async_copy(w_x, weight_grad_hbm.reshape(w_x.shape), local_sems.at[4])
    weight_grad_copy.start()
    arrived(xb_in, far_back)
    feat_grad[...] = (mine + xb_in[...].astype(F32)).astype(BF)
    feat_grad_copy = pltpu.make_async_copy(feat_grad, feat_grad_hbm.at[0], local_sems.at[5])
    feat_grad_copy.start()
    for copy in pending:
        copy.wait_send()
    layer_copy.wait()
    weight_grad_copy.wait()
    feat_grad_copy.wait()
    assert counters["send"] <= send_sems.shape[0] and counters["recv"] <= recv_sems.shape[0]


def write_outputs(
    layer_out, feat_grad, weight_grad, layer_hbm, feat_grad_hbm, weight_grad_hbm, layer_buf, feat_grad_buf, weight_buf, sems
):
    rows = weight_buf.shape[0] // 4
    jobs = [(feat_grad, feat_grad_buf, feat_grad_hbm), (layer_out, layer_buf, layer_hbm)]
    for i in range(4):
        at = pl.ds(i * rows, rows)
        jobs.append((weight_grad.at[at], weight_buf.at[at], weight_grad_hbm.at[at]))
    reads = [pltpu.make_async_copy(src, buf, sems.at[0, i]) for i, (src, buf, _) in enumerate(jobs)]
    writes = [pltpu.make_async_copy(buf, dst, sems.at[1, i]) for i, (_, buf, dst) in enumerate(jobs)]
    for read in reads:
        read.start()
    for read, write in zip(reads, writes):
        read.wait()
        write.start()
    for write in writes:
        write.wait()


def local(n_row, n_col, feats, weight, cotangent, tile_values, tile_rows, tile_cols, tile_count):
    rows_here, width = feats.shape[1:]
    slots = tile_values.shape[2]
    Y, Z, X = n_row // X_HI, n_col // (X_LO * CORE), X_HI * X_LO
    row_tiles, col_tiles = n_col, n_row
    ids = tile_rows[0, 0] * col_tiles + tile_cols[0, 0]
    slot_ids = jnp.arange(slots, dtype=jnp.int32)
    ids = jnp.where(slot_ids < tile_count[0, 0], ids, -1)
    places = jnp.arange(row_tiles * col_tiles, dtype=jnp.int32)
    hit = ids[None, :] == places[:, None]
    tab = jnp.min(jnp.where(hit, slot_ids[None, :], slots), axis=1)

    block = (128, width)
    w_rows = width // (CORE * Y * X)
    w_full = (CORE, Y, X, 2, w_rows // 2, width)
    scratch = [
        pltpu.VMEM((width, width), BF),
        pltpu.VMEM(block, BF),
        pltpu.VMEM(block, BF),
        pltpu.VMEM(block, BF),
        pltpu.VMEM((slots + 1, 128, 128), BF),
        pltpu.VMEM((row_tiles * 128, col_tiles * 128), BF),
        pltpu.VMEM((n_row,) + block, BF),
        pltpu.VMEM((Z, X_LO, CORE) + block, BF),
        pltpu.VMEM((Z, X_LO) + block, BF),
        pltpu.VMEM((Z // 2, 2) + block, BF),
        pltpu.VMEM((Z // 2, 2) + block, BF),
        pltpu.VMEM(block, BF),
        pltpu.VMEM(block, BF),
        pltpu.VMEM((Z, X_LO, CORE) + block, BF),
        pltpu.VMEM((col_tiles * 128, width), F32),
        pltpu.VMEM((X_HI, Y) + block, BF),
        pltpu.VMEM((Y // 2, 2) + block, BF),
        pltpu.VMEM((Y // 2, 2) + block, BF),
        pltpu.VMEM(block, BF),
        pltpu.VMEM((CORE, Y, 2, X * w_rows // 2, width), F32),
        pltpu.VMEM((Y, 2, X * w_rows // 2, width), F32),
        pltpu.VMEM((Y // 2, 2, X * w_rows // 2, width), F32),
        pltpu.VMEM((Y // 2, 2, X * w_rows // 2, width), F32),
        pltpu.VMEM((2, X // 2, 2, w_rows // 2, width), F32),
        pltpu.VMEM((X // 2, 2, w_rows // 2, width), F32),
        pltpu.VMEM((X // 2, 2, w_rows // 2, width), F32),
        pltpu.VMEM(w_full, F32),
        pltpu.VMEM((Z, 2, w_rows // 2, width), F32),
        pltpu.SemaphoreType.DMA,
        pltpu.SemaphoreType.DMA((6,)),
        pltpu.SemaphoreType.DMA((180,)),
        pltpu.SemaphoreType.DMA((210,)),
        pltpu.SemaphoreType.DMA((Z,)),
        pltpu.SemaphoreType.DMA((Z,)),
    ]
    hbm = pl.BlockSpec(memory_space=pltpu.HBM)
    layer_out, feat_grad, weight_grad = pl.pallas_call(
        functools.partial(layer_kernel, n_row, n_col),
        out_shape=(
            jax.ShapeDtypeStruct((1,) + block, BF),
            jax.ShapeDtypeStruct((1,) + block, BF),
            jax.ShapeDtypeStruct((width, width), F32),
        ),
        in_specs=[pl.BlockSpec(memory_space=pltpu.SMEM), hbm, hbm, hbm, hbm],
        out_specs=(hbm, hbm, hbm),
        scratch_shapes=scratch,
        compiler_params=pltpu.CompilerParams(
            collective_id=0, has_side_effects=True, vmem_limit_bytes=60 * 1024 * 1024
        ),
    )(tab, feats, weight, cotangent, tile_values)
    return pl.pallas_call(
        write_outputs,
        out_shape=(
            jax.ShapeDtypeStruct((1,) + block, BF),
            jax.ShapeDtypeStruct((1,) + block, BF),
            jax.ShapeDtypeStruct((width, width), F32),
        ),
        in_specs=[hbm, hbm, hbm],
        out_specs=(hbm, hbm, hbm),
        scratch_shapes=[
            pltpu.VMEM((1,) + block, BF),
            pltpu.VMEM((1,) + block, BF),
            pltpu.VMEM((width, width), F32),
            pltpu.SemaphoreType.DMA((2, 6)),
        ],
    )(layer_out, feat_grad, weight_grad)


def solution(mesh):
    in_specs = (
        P("col", "row", None),
        P(),
        P("row", "col", None),
        P("row", "col", None, None, None),
        P("row", "col", None),
        P("row", "col", None),
        P("row", "col"),
    )
    out_specs = (P("row", "col", None), P("col", "row", None), P())
    return jax.shard_map(
        functools.partial(local, mesh.shape["row"], mesh.shape["col"]),
        mesh=mesh, in_specs=in_specs, out_specs=out_specs, check_vma=False,
    )
```

```python
import functools

import jax
import jax.numpy as jnp
from jax import lax
from jax.experimental import pallas as pl
from jax.experimental.pallas import tpu as pltpu
from jax.sharding import PartitionSpec as P

BF = jnp.bfloat16
F32 = jnp.float32
X_HI, X_LO, CORE = 2, 2, 2


def layer_kernel(
    n_row, n_col, tab, feats_hbm, weight_hbm, cot_hbm, tiles_hbm, layer_hbm, feat_grad_hbm, weight_grad_hbm,
    weight, cot, layer_out, feat_grad, tiles, dense, panel, part, core_in, rp, rm, own_sum, x_in, gath, acc, back, yp, ym, xb_in,
    w_term, w_core, wy_p, wy_m, w_y, wx_p, wx_m, w_x, w_z,
    tile_sem, local_sems, send_sems, recv_sems, core_send, core_recv,
):
    Y, Z = n_row // X_HI, n_col // (X_LO * CORE)
    X = X_HI * X_LO
    HZ = Z // 2
    slots = tiles_hbm.shape[2]
    row_tiles, col_tiles = n_col, n_row
    chunk = row_tiles * 128 // Z
    width = feats_hbm.shape[2]
    half_rows = 64

    r, c = lax.axis_index("row"), lax.axis_index("col")
    xh, y = r // Y, r % Y
    z, xl, k = c // (X_LO * CORE), (c // CORE) % X_LO, c % CORE
    x = xh * X_LO + xl

    def device(x_at, y_at, z_at, k_at):
        return ((x_at // X_LO) * Y + y_at, z_at * (X_LO * CORE) + (x_at % X_LO) * CORE + k_at)

    core_dev = device(x, y, z, 1 - k)
    x_plus, x_minus = device((x + 1) % X, y, z, k), device((x + X - 1) % X, y, z, k)
    x_far = device((x + 2) % X, y, z, k)
    x_near = device(xh * X_LO + 1 - xl, y, z, k)
    y_plus, y_minus = device(x, (y + 1) % Y, z, k), device(x, (y + Y - 1) % Y, z, k)
    z_plus, z_minus = device(x, y, (z + 1) % Z, k), device(x, y, (z + Z - 1) % Z, k)

    pending = []
    counters = {"send": 0, "recv": 0}

    def fresh():
        counters["recv"] += 1
        return counters["recv"] - 1

    def remote(src, dst, sem_out, sem_in, dev):
        return pltpu.make_async_remote_copy(
            src_ref=src, dst_ref=dst, send_sem=sem_out, recv_sem=sem_in,
            device_id=dev, device_id_type=pl.DeviceIdType.MESH,
        )

    def send(src, dst, sem, dev):
        copy = remote(src, dst, send_sems.at[counters["send"]], recv_sems.at[sem], dev)
        counters["send"] += 1
        copy.start()
        pending.append(copy)

    def arrived(view, sem):
        remote(view, view, send_sems.at[0], recv_sems.at[sem], core_dev).wait_recv()

    def add_into(dst, other):
        dst[...] = (dst[...].astype(F32) + other[...].astype(F32)).astype(dst.dtype)

    def ring_gather(pos, n, view, plus, minus, ready=None, on_block=None):
        half = n // 2
        sems = {(s, d, o): fresh() for s in (1, -1) for d in range(1, half + 1) for o in (0, 1)}

        def goes(s, d, o):
            return d < half or (d == half and o == (0 if s == 1 else 1))

        for o in (0, 1):
            if ready is not None:
                ready(o)
            for s in (1, -1):
                if goes(s, 1, o):
                    send(view(pos, o), view(pos, o), sems[s, 1, o], plus if s == 1 else minus)
        for d in range(1, half + 1):
            yield
            for o in (0, 1):
                for s in (1, -1):
                    if not goes(s, d, o):
                        continue
                    at = (pos - s * d + n) % n
                    arrived(view(at, o), sems[s, d, o])
                    if goes(s, d + 1, o):
                        send(view(at, o), view(at, o), sems[s, d + 1, o], plus if s == 1 else minus)
                    if on_block is not None:
                        on_block(at, o, s, d)

    def ring_sum(pos, n, view, bufs_p, bufs_m, plus, minus, before=None, middle=None, defer=False):
        half = n // 2
        bufs, dev = {1: bufs_p, -1: bufs_m}, {1: plus, -1: minus}
        sems = {(s, d, o): fresh() for s in (1, -1) for d in range(half) for o in (0, 1)}
        first = {(1, 0): half, (1, 1): half - 1, (-1, 1): half, (-1, 0): half - 1}
        for o in (0, 1):
            for s in (1, -1):
                d = first[s, o]
                if d > 0 and d == half:
                    send(view((pos + s * d + n) % n, o), bufs[s].at[d - 1, o], sems[s, d - 1, o], dev[s])
        if middle is not None:
            middle()

        def second(s, o):
            d = first[s, o]
            if d > 0 and d < half:
                send(view((pos + s * d + n) % n, o), bufs[s].at[d - 1, o], sems[s, d - 1, o], dev[s])

        for o in (1, 0):
            for s in (1, -1):
                if not (defer and (s, o) == (-1, 0)):
                    second(s, o)
        for d in range(half - 1, 0, -1):
            yield
            if before is not None:
                before(d)
            for o in (1, 0):
                for s in (1, -1):
                    if d >= first[s, o]:
                        continue
                    buf = bufs[s].at[d, o]
                    arrived(buf, sems[s, d, o])
                    add_into(buf, view((pos + s * d + n) % n, o))
                    send(buf, bufs[s].at[d - 1, o], sems[s, d - 1, o], dev[s])
                    if defer and d == half - 1 and (s, o) == (-1, 1):
                        second(-1, 0)
        yield
        if before is not None:
            before(0)

        def total(o):
            value = view(pos, o)[...].astype(F32)
            for s in (1, -1):
                if first[s, o] > 0:
                    arrived(bufs[s].at[0, o], sems[s, 0, o])
                    value = value + bufs[s][0, o].astype(F32)
            return value

        return total

    def panel_at(at, o):
        return panel.at[(xh if o == 0 else 1 - xh) * Y + at]

    feats_copy = pltpu.make_async_copy(feats_hbm.at[0], panel_at(y, 0), local_sems.at[0])
    feats_copy.start()
    weight_copy = pltpu.make_async_copy(weight_hbm, weight, local_sems.at[1])
    cot_copy = pltpu.make_async_copy(cot_hbm.at[0], cot, local_sems.at[2])
    tile_copy = pltpu.make_async_copy(tiles_hbm.at[0, 0], tiles.at[pl.ds(0, slots)], tile_sem)
    tile_copy.start()
    barrier = pltpu.get_barrier_semaphore()
    peers = (core_dev, x_plus, x_minus, x_far, y_plus, y_minus, z_plus, z_minus)
    for dev in peers:
        pl.semaphore_signal(barrier, inc=1, device_id=dev, device_id_type=pl.DeviceIdType.MESH)
    weight_copy.start()
    cot_copy.start()
    tiles[slots] = jnp.zeros(tiles.shape[1:], tiles.dtype)
    feats_copy.wait()
    pl.semaphore_wait(barrier, len(peers))

    far_sem = fresh()
    send(panel_at(y, 0), panel_at(y, 0), far_sem, x_far)

    def densify():
        tile_copy.wait()

        def one_row(i, carry):
            for j in range(col_tiles):
                dense[pl.ds(pl.multiple_of(i * 128, 128), 128), j * 128 : (j + 1) * 128] = tiles[tab[i * col_tiles + j]]
            return carry

        lax.fori_loop(0, row_tiles, one_row, 0)

    def panel_ready(o):
        if o == 1:
            densify()
            arrived(panel_at(y, 1), far_sem)

    for _ in ring_gather(y, Y, panel_at, y_plus, y_minus, ready=panel_ready):
        pass

    def forward_chunk(t, carry):
        off = HZ + (1 - 2 * (t % 2)) * ((t + 1) // 2)
        at = (z + off) % Z
        product = jnp.dot(
            dense[pl.ds(pl.multiple_of(at * chunk, chunk), chunk), :],
            panel[...].reshape(col_tiles * 128, width),
            preferred_element_type=F32,
        )
        part[at] = product.astype(BF).reshape(X_LO, CORE, 128, width)
        remote(
            part.at[at, :, 1 - k], core_in.at[at], core_send.at[t], core_recv.at[t], core_dev
        ).start()
        return carry

    def core_total(t):
        off = HZ + (1 - 2 * (t % 2)) * ((t + 1) // 2)
        at = (z + off) % Z
        remote(
            part.at[at, :, 1 - k], core_in.at[at], core_send.at[t], core_recv.at[t], core_dev
        ).wait()
        for o in range(X_LO):
            add_into(core_in.at[at, o], part.at[at, o, k])

    def sum_at(at, o):
        return core_in.at[at, xl if o == 0 else 1 - xl]

    lax.fori_loop(0, 2, forward_chunk, 0)
    core_total(0)

    def middle():
        forward_chunk(2, 0)
        core_total(1)
        core_total(2)

    done = [3]

    def before(d):
        if d == HZ - 1:
            lax.fori_loop(3, Z, forward_chunk, 0)
        while done[0] < Z and d <= HZ - 2 and done[0] <= 2 * (HZ - d):
            core_total(done[0])
            done[0] += 1

    steps = ring_sum(z, Z, sum_at, rp, rm, z_plus, z_minus, before=before, middle=middle)
    while True:
        try:
            next(steps)
        except StopIteration as stop:
            total = stop.value
            break
    x_sem = fresh()
    own_sum[...] = total(1).astype(BF)
    send(own_sum, x_in, x_sem, x_near)
    mine = total(0)
    arrived(x_in, x_sem)
    summed = (mine + x_in[...].astype(F32)).astype(BF)

    weight_copy.wait()
    cot_copy.wait()
    hidden = jnp.dot(summed, weight[...], preferred_element_type=F32)
    gate = jax.nn.sigmoid(hidden)
    hidden_grad = (cot[...].astype(F32) * gate * (1.0 + hidden * (1.0 - gate))).astype(BF)
    grad_rows = lax.dot_general(
        hidden_grad, weight[...], (((1,), (1,)), ((), ())), preferred_element_type=F32
    ).astype(BF)
    gath[z, xl, k] = grad_rows

    def piece(at, p, core):
        slot = xl if p == 0 else 1 - xl
        if p == 0:
            return gath.at[at, slot, core]
        return gath.at[at, slot, core, pl.ds((p - 1) * half_rows, half_rows)]

    def own_half(at, h):
        return gath.at[at, xl, k, pl.ds(h * half_rows, half_rows)]

    pair_sems, near_sems = {}, {}

    def to_core(at, p, s, d):
        pair_sems[p, s, d] = fresh()
        send(piece(at, p, k), piece(at, p, k), pair_sems[p, s, d], core_dev)

    def to_near(at, h, s, d):
        near_sems[h, s, d] = fresh()
        send(own_half(at, h), own_half(at, h), near_sems[h, s, d], x_near)

    def from_near(at, h, s, d):
        arrived(piece(at, 1 + h, k), near_sems[h, s, d])

    to_near(z, 0, 1, 0)
    layer_copy = pltpu.make_async_copy(layer_out, layer_hbm.at[0], local_sems.at[3])

    def gath_ready(o):
        if o == 1:
            to_near(z, 1, 1, 0)
            to_core(z, 0, 1, 0)
            layer_out[...] = (hidden * gate).astype(BF)
            layer_copy.start()
            w_term[...] = (
                lax.dot_general(summed, hidden_grad, (((0,), (0,)), ((), ())), preferred_element_type=F32)
                * (n_row * n_col * 128) ** (-0.5)
            ).reshape(w_term.shape)
            from_near(z, 0, 1, 0)

    def gath_block(at, o, s, d):
        if o == 0 and d < HZ:
            to_near(at, 1, s, d)
        to_core(at, o, s, d)

    last_sem = fresh()

    def backward_chunk(at):
        product = lax.dot_general(
            dense[pl.ds(pl.multiple_of(at * chunk, chunk), chunk), :],
            gath[at].reshape(chunk, width),
            (((0,), (0,)), ((), ())),
            preferred_element_type=F32,
        )
        return product

    def accumulate(keys, at, start=False):
        for p, s, d in keys:
            arrived(piece(at, p, 1 - k), pair_sems[p, s, d])
        if start:
            acc[...] = backward_chunk(at)
        else:
            acc[...] += backward_chunk(at)

    def weight_steps():
        sem = fresh()
        send(w_term.at[1 - k], w_core, sem, core_dev)
        yield
        arrived(w_core, sem)
        add_into(w_core, w_term.at[k])
        total = yield from ring_sum(
            y, Y, lambda at, o: w_core.at[at, o], wy_p, wy_m, y_plus, y_minus
        )
        for o in (0, 1):
            w_y[o] = total(o).reshape(w_y.shape[1:])
        total = yield from ring_sum(
            x, X, lambda at, o: w_y.at[at // 2, at % 2, o], wx_p, wx_m, x_plus, x_minus
        )
        for o in (0, 1):
            w_z[z, o] = total(o)
        yield from ring_gather(z, Z, lambda at, o: w_z.at[at, o], z_plus, z_minus)
        full = w_z[0]
        for at in range(1, Z):
            full = full + w_z[at]
        w_x[k, y, x] = full
        yield from ring_gather(x, X, lambda at, o: w_x.at[k, y, at, o], x_plus, x_minus)
        yield from ring_gather(
            y, Y, lambda at, o: w_x.at[k, at, pl.ds(o * (X // 2), X // 2)], y_plus, y_minus
        )
        sem = fresh()
        send(w_x.at[k], w_x.at[k], sem, core_dev)
        yield
        arrived(w_x.at[1 - k], sem)

    weight_run = weight_steps()

    def weight_step(count):
        for _ in range(count):
            next(weight_run, None)

    gather_run = ring_gather(
        z, Z, lambda at, o: piece(at, o, k), z_plus, z_minus, ready=gath_ready, on_block=gath_block
    )
    next(gather_run)
    to_core(z, 1, 1, 0)
    weight_step(1)
    from_near(z, 1, 1, 0)
    to_core(z, 2, 1, 0)
    weight_step(1)
    for d in range(1, HZ + 1):
        next(gather_run, None)
        weight_step(1)
        if d == 1:
            accumulate([(p, 1, 0) for p in range(3)], z, start=True)
        else:
            for s in (1, -1):
                accumulate([(p, s, d - 1) for p in range(3)], (z - s * (d - 1) + Z) % Z)
        weight_step(1)
        if d < HZ:
            for s in (-1, 1):
                at = (z - s * d + Z) % Z
                from_near(at, 1, s, d)
                if d == HZ - 1 and s == -1:
                    send(piece(at, 2, k), piece(at, 2, k), last_sem, z_minus)
                to_core(at, 2, s, d)
    far = (z + HZ) % Z
    arrived(piece(far, 2, k), last_sem)
    to_core(far, 2, -1, HZ)
    accumulate([(0, 1, HZ), (1, -1, HZ), (2, -1, HZ)], far)

    back[...] = acc[...].astype(BF).reshape(back.shape)

    def back_at(at, o):
        return back.at[xh if o == 0 else 1 - xh, at]

    steps = ring_sum(y, Y, back_at, yp, ym, y_plus, y_minus, defer=True)
    while True:
        try:
            next(steps)
            weight_step(1)
        except StopIteration as stop:
            total = stop.value
            break
    far_back = fresh()
    own_sum2 = yp.at[1, 1]
    own_sum2[...] = total(1).astype(BF)
    send(own_sum2, xb_in, far_back, x_far)
    mine = total(0)
    for _ in weight_run:
        pass
    weight_grad_copy = pltpu.make_async_copy(w_x, weight_grad_hbm.reshape(w_x.shape), local_sems.at[4])
    weight_grad_copy.start()
    arrived(xb_in, far_back)
    feat_grad[...] = (mine + xb_in[...].astype(F32)).astype(BF)
    feat_grad_copy = pltpu.make_async_copy(feat_grad, feat_grad_hbm.at[0], local_sems.at[5])
    feat_grad_copy.start()
    for copy in pending:
        copy.wait_send()
    layer_copy.wait()
    weight_grad_copy.wait()
    feat_grad_copy.wait()
    assert counters["send"] <= send_sems.shape[0] and counters["recv"] <= recv_sems.shape[0]


def write_outputs(
    layer_out, feat_grad, weight_grad, layer_hbm, feat_grad_hbm, weight_grad_hbm, layer_buf, feat_grad_buf, weight_buf, sems
):
    rows = weight_buf.shape[0] // 4
    jobs = [(feat_grad, feat_grad_buf, feat_grad_hbm), (layer_out, layer_buf, layer_hbm)]
    for i in range(4):
        at = pl.ds(i * rows, rows)
        jobs.append((weight_grad.at[at], weight_buf.at[at], weight_grad_hbm.at[at]))
    reads = [pltpu.make_async_copy(src, buf, sems.at[0, i]) for i, (src, buf, _) in enumerate(jobs)]
    writes = [pltpu.make_async_copy(buf, dst, sems.at[1, i]) for i, (_, buf, dst) in enumerate(jobs)]
    for read in reads:
        read.start()
    for read, write in zip(reads, writes):
        read.wait()
        write.start()
    for write in writes:
        write.wait()


def local(n_row, n_col, feats, weight, cotangent, tile_values, tile_rows, tile_cols, tile_count):
    rows_here, width = feats.shape[1:]
    slots = tile_values.shape[2]
    Y, Z, X = n_row // X_HI, n_col // (X_LO * CORE), X_HI * X_LO
    row_tiles, col_tiles = n_col, n_row
    ids = tile_rows[0, 0] * col_tiles + tile_cols[0, 0]
    slot_ids = jnp.arange(slots, dtype=jnp.int32)
    ids = jnp.where(slot_ids < tile_count[0, 0], ids, -1)
    places = jnp.arange(row_tiles * col_tiles, dtype=jnp.int32)
    hit = ids[None, :] == places[:, None]
    tab = jnp.min(jnp.where(hit, slot_ids[None, :], slots), axis=1)

    block = (128, width)
    w_rows = width // (CORE * Y * X)
    w_full = (CORE, Y, X, 2, w_rows // 2, width)
    scratch = [
        pltpu.VMEM((width, width), BF),
        pltpu.VMEM(block, BF),
        pltpu.VMEM(block, BF),
        pltpu.VMEM(block, BF),
        pltpu.VMEM((slots + 1, 128, 128), BF),
        pltpu.VMEM((row_tiles * 128, col_tiles * 128), BF),
        pltpu.VMEM((n_row,) + block, BF),
        pltpu.VMEM((Z, X_LO, CORE) + block, BF),
        pltpu.VMEM((Z, X_LO) + block, BF),
        pltpu.VMEM((Z // 2, 2) + block, BF),
        pltpu.VMEM((Z // 2, 2) + block, BF),
        pltpu.VMEM(block, BF),
        pltpu.VMEM(block, BF),
        pltpu.VMEM((Z, X_LO, CORE) + block, BF),
        pltpu.VMEM((col_tiles * 128, width), F32),
        pltpu.VMEM((X_HI, Y) + block, BF),
        pltpu.VMEM((Y // 2, 2) + block, BF),
        pltpu.VMEM((Y // 2, 2) + block, BF),
        pltpu.VMEM(block, BF),
        pltpu.VMEM((CORE, Y, 2, X * w_rows // 2, width), F32),
        pltpu.VMEM((Y, 2, X * w_rows // 2, width), F32),
        pltpu.VMEM((Y // 2, 2, X * w_rows // 2, width), F32),
        pltpu.VMEM((Y // 2, 2, X * w_rows // 2, width), F32),
        pltpu.VMEM((2, X // 2, 2, w_rows // 2, width), F32),
        pltpu.VMEM((X // 2, 2, w_rows // 2, width), F32),
        pltpu.VMEM((X // 2, 2, w_rows // 2, width), F32),
        pltpu.VMEM(w_full, F32),
        pltpu.VMEM((Z, 2, w_rows // 2, width), F32),
        pltpu.SemaphoreType.DMA,
        pltpu.SemaphoreType.DMA((6,)),
        pltpu.SemaphoreType.DMA((180,)),
        pltpu.SemaphoreType.DMA((210,)),
        pltpu.SemaphoreType.DMA((Z,)),
        pltpu.SemaphoreType.DMA((Z,)),
    ]
    hbm = pl.BlockSpec(memory_space=pltpu.HBM)
    layer_out, feat_grad, weight_grad = pl.pallas_call(
        functools.partial(layer_kernel, n_row, n_col),
        out_shape=(
            jax.ShapeDtypeStruct((1,) + block, BF),
            jax.ShapeDtypeStruct((1,) + block, BF),
            jax.ShapeDtypeStruct((width, width), F32),
        ),
        in_specs=[pl.BlockSpec(memory_space=pltpu.SMEM), hbm, hbm, hbm, hbm],
        out_specs=(hbm, hbm, hbm),
        scratch_shapes=scratch,
        compiler_params=pltpu.CompilerParams(
            collective_id=0, has_side_effects=True, vmem_limit_bytes=60 * 1024 * 1024
        ),
    )(tab, feats, weight, cotangent, tile_values)
    return pl.pallas_call(
        write_outputs,
        out_shape=(
            jax.ShapeDtypeStruct((1,) + block, BF),
            jax.ShapeDtypeStruct((1,) + block, BF),
            jax.ShapeDtypeStruct((width, width), F32),
        ),
        in_specs=[hbm, hbm, hbm],
        out_specs=(hbm, hbm, hbm),
        scratch_shapes=[
            pltpu.VMEM((1,) + block, BF),
            pltpu.VMEM((1,) + block, BF),
            pltpu.VMEM((width, width), F32),
            pltpu.SemaphoreType.DMA((2, 6)),
        ],
    )(layer_out, feat_grad, weight_grad)


def solution(mesh):
    in_specs = (
        P("col", "row", None),
        P(),
        P("row", "col", None),
        P("row", "col", None, None, None),
        P("row", "col", None),
        P("row", "col", None),
        P("row", "col"),
    )
    out_specs = (P("row", "col", None), P("col", "row", None), P())
    return jax.shard_map(
        functools.partial(local, mesh.shape["row"], mesh.shape["col"]),
        mesh=mesh, in_specs=in_specs, out_specs=out_specs, check_vma=False,
    )
```

```python
import functools

import jax
import jax.numpy as jnp
from jax import lax
from jax.experimental import pallas as pl
from jax.experimental.pallas import tpu as pltpu
from jax.sharding import PartitionSpec as P

BF = jnp.bfloat16
F32 = jnp.float32
X_HI, X_LO, CORE = 2, 2, 2


def layer_kernel(
    n_row, n_col, tab, feats_hbm, weight_hbm, cot_hbm, tiles_hbm, layer_hbm, feat_grad_hbm, weight_grad_hbm,
    weight, cot, layer_out, feat_grad, tiles, dense, panel, part, core_in, rp, rm, own_sum, x_in, gath, acc, back, yp, ym, xb_in,
    w_term, w_core, wy_p, wy_m, w_y, wx_p, wx_m, w_x, w_z,
    tile_sem, local_sems, send_sems, recv_sems, core_send, core_recv,
):
    Y, Z = n_row // X_HI, n_col // (X_LO * CORE)
    X = X_HI * X_LO
    HZ = Z // 2
    slots = tiles_hbm.shape[2]
    row_tiles, col_tiles = n_col, n_row
    chunk = row_tiles * 128 // Z
    width = feats_hbm.shape[2]
    half_rows = 64

    r, c = lax.axis_index("row"), lax.axis_index("col")
    xh, y = r // Y, r % Y
    z, xl, k = c // (X_LO * CORE), (c // CORE) % X_LO, c % CORE
    x = xh * X_LO + xl

    def device(x_at, y_at, z_at, k_at):
        return ((x_at // X_LO) * Y + y_at, z_at * (X_LO * CORE) + (x_at % X_LO) * CORE + k_at)

    core_dev = device(x, y, z, 1 - k)
    x_plus, x_minus = device((x + 1) % X, y, z, k), device((x + X - 1) % X, y, z, k)
    x_far = device((x + 2) % X, y, z, k)
    x_near = device(xh * X_LO + 1 - xl, y, z, k)
    y_plus, y_minus = device(x, (y + 1) % Y, z, k), device(x, (y + Y - 1) % Y, z, k)
    z_plus, z_minus = device(x, y, (z + 1) % Z, k), device(x, y, (z + Z - 1) % Z, k)

    pending = []
    counters = {"send": 0, "recv": 0}

    def fresh():
        counters["recv"] += 1
        return counters["recv"] - 1

    def remote(src, dst, sem_out, sem_in, dev):
        return pltpu.make_async_remote_copy(
            src_ref=src, dst_ref=dst, send_sem=sem_out, recv_sem=sem_in,
            device_id=dev, device_id_type=pl.DeviceIdType.MESH,
        )

    def send(src, dst, sem, dev):
        copy = remote(src, dst, send_sems.at[counters["send"]], recv_sems.at[sem], dev)
        counters["send"] += 1
        copy.start()
        pending.append(copy)

    def arrived(view, sem):
        remote(view, view, send_sems.at[0], recv_sems.at[sem], core_dev).wait_recv()

    def add_into(dst, other):
        dst[...] = (dst[...].astype(F32) + other[...].astype(F32)).astype(dst.dtype)

    def ring_gather(pos, n, view, plus, minus, ready=None, on_block=None):
        half = n // 2
        sems = {(s, d, o): fresh() for s in (1, -1) for d in range(1, half + 1) for o in (0, 1)}

        def goes(s, d, o):
            return d < half or (d == half and o == (0 if s == 1 else 1))

        for o in (0, 1):
            if ready is not None:
                ready(o)
            for s in (1, -1):
                if goes(s, 1, o):
                    send(view(pos, o), view(pos, o), sems[s, 1, o], plus if s == 1 else minus)
        for d in range(1, half + 1):
            yield
            for o in (0, 1):
                for s in (1, -1):
                    if not goes(s, d, o):
                        continue
                    at = (pos - s * d + n) % n
                    arrived(view(at, o), sems[s, d, o])
                    if goes(s, d + 1, o):
                        send(view(at, o), view(at, o), sems[s, d + 1, o], plus if s == 1 else minus)
                    if on_block is not None:
                        on_block(at, o, s, d)

    def ring_sum(pos, n, view, bufs_p, bufs_m, plus, minus, before=None):
        half = n // 2
        bufs, dev = {1: bufs_p, -1: bufs_m}, {1: plus, -1: minus}
        sems = {(s, d, o): fresh() for s in (1, -1) for d in range(half) for o in (0, 1)}
        first = {(1, 0): half, (1, 1): half - 1, (-1, 1): half, (-1, 0): half - 1}
        for o in (0, 1):
            for s in (1, -1):
                d = first[s, o]
                if d > 0 and d == half:
                    send(view((pos + s * d + n) % n, o), bufs[s].at[d - 1, o], sems[s, d - 1, o], dev[s])
        for o in (1, 0):
            for s in (1, -1):
                d = first[s, o]
                if d > 0 and d < half:
                    send(view((pos + s * d + n) % n, o), bufs[s].at[d - 1, o], sems[s, d - 1, o], dev[s])
        for d in range(half - 1, 0, -1):
            yield
            if before is not None:
                before(d)
            for o in (1, 0):
                for s in (1, -1):
                    if d >= first[s, o]:
                        continue
                    buf = bufs[s].at[d, o]
                    arrived(buf, sems[s, d, o])
                    add_into(buf, view((pos + s * d + n) % n, o))
                    send(buf, bufs[s].at[d - 1, o], sems[s, d - 1, o], dev[s])
        yield
        if before is not None:
            before(0)

        def total(o):
            value = view(pos, o)[...].astype(F32)
            for s in (1, -1):
                if first[s, o] > 0:
                    arrived(bufs[s].at[0, o], sems[s, 0, o])
                    value = value + bufs[s][0, o].astype(F32)
            return value

        return total

    def panel_at(at, o):
        return panel.at[(xh if o == 0 else 1 - xh) * Y + at]

    feats_copy = pltpu.make_async_copy(feats_hbm.at[0], panel_at(y, 0), local_sems.at[0])
    feats_copy.start()
    weight_copy = pltpu.make_async_copy(weight_hbm, weight, local_sems.at[1])
    cot_copy = pltpu.make_async_copy(cot_hbm.at[0], cot, local_sems.at[2])
    tile_copy = pltpu.make_async_copy(tiles_hbm.at[0, 0], tiles.at[pl.ds(0, slots)], tile_sem)
    tile_copy.start()
    barrier = pltpu.get_barrier_semaphore()
    peers = (core_dev, x_plus, x_minus, x_far, y_plus, y_minus, z_plus, z_minus)
    for dev in peers:
        pl.semaphore_signal(barrier, inc=1, device_id=dev, device_id_type=pl.DeviceIdType.MESH)
    weight_copy.start()
    cot_copy.start()
    tiles[slots] = jnp.zeros(tiles.shape[1:], tiles.dtype)
    feats_copy.wait()
    pl.semaphore_wait(barrier, len(peers))

    far_sem = fresh()
    send(panel_at(y, 0), panel_at(y, 0), far_sem, x_far)

    def densify():
        tile_copy.wait()

        def one_row(i, carry):
            for j in range(col_tiles):
                dense[pl.ds(pl.multiple_of(i * 128, 128), 128), j * 128 : (j + 1) * 128] = tiles[tab[i * col_tiles + j]]
            return carry

        lax.fori_loop(0, row_tiles, one_row, 0)

    def panel_ready(o):
        if o == 1:
            densify()
            arrived(panel_at(y, 1), far_sem)

    for _ in ring_gather(y, Y, panel_at, y_plus, y_minus, ready=panel_ready):
        pass

    def forward_chunk(t, carry):
        off = HZ + (1 - 2 * (t % 2)) * ((t + 1) // 2)
        at = (z + off) % Z
        product = jnp.dot(
            dense[pl.ds(pl.multiple_of(at * chunk, chunk), chunk), :],
            panel[...].reshape(col_tiles * 128, width),
            preferred_element_type=F32,
        )
        part[at] = product.astype(BF).reshape(X_LO, CORE, 128, width)
        remote(
            part.at[at, :, 1 - k], core_in.at[at], core_send.at[t], core_recv.at[t], core_dev
        ).start()
        return carry

    def core_total(t):
        off = HZ + (1 - 2 * (t % 2)) * ((t + 1) // 2)
        at = (z + off) % Z
        remote(
            part.at[at, :, 1 - k], core_in.at[at], core_send.at[t], core_recv.at[t], core_dev
        ).wait()
        for o in range(X_LO):
            add_into(core_in.at[at, o], part.at[at, o, k])

    def sum_at(at, o):
        return core_in.at[at, xl if o == 0 else 1 - xl]

    lax.fori_loop(0, 3, forward_chunk, 0)
    for t in range(3):
        core_total(t)

    done = [3]

    def before(d):
        if d == HZ - 1:
            lax.fori_loop(3, Z, forward_chunk, 0)
        while done[0] < Z and d <= HZ - 2 and done[0] <= 2 * (HZ - d):
            core_total(done[0])
            done[0] += 1

    steps = ring_sum(z, Z, sum_at, rp, rm, z_plus, z_minus, before=before)
    while True:
        try:
            next(steps)
        except StopIteration as stop:
            total = stop.value
            break
    x_sem = fresh()
    own_sum[...] = total(1).astype(BF)
    send(own_sum, x_in, x_sem, x_near)
    mine = total(0)
    arrived(x_in, x_sem)
    summed = (mine + x_in[...].astype(F32)).astype(BF)

    weight_copy.wait()
    cot_copy.wait()
    hidden = jnp.dot(summed, weight[...], preferred_element_type=F32)
    gate = jax.nn.sigmoid(hidden)
    hidden_grad = (cot[...].astype(F32) * gate * (1.0 + hidden * (1.0 - gate))).astype(BF)
    grad_rows = lax.dot_general(
        hidden_grad, weight[...], (((1,), (1,)), ((), ())), preferred_element_type=F32
    ).astype(BF)
    gath[z, xl, k] = grad_rows

    def piece(at, p, core):
        slot = xl if p == 0 else 1 - xl
        if p == 0:
            return gath.at[at, slot, core]
        return gath.at[at, slot, core, pl.ds((p - 1) * half_rows, half_rows)]

    def own_half(at, h):
        return gath.at[at, xl, k, pl.ds(h * half_rows, half_rows)]

    pair_sems, near_sems = {}, {}

    def to_core(at, p, s, d):
        pair_sems[p, s, d] = fresh()
        send(piece(at, p, k), piece(at, p, k), pair_sems[p, s, d], core_dev)

    def to_near(at, h, s, d):
        near_sems[h, s, d] = fresh()
        send(own_half(at, h), own_half(at, h), near_sems[h, s, d], x_near)

    def from_near(at, h, s, d):
        arrived(piece(at, 1 + h, k), near_sems[h, s, d])

    to_near(z, 0, 1, 0)
    layer_copy = pltpu.make_async_copy(layer_out, layer_hbm.at[0], local_sems.at[3])

    def gath_ready(o):
        if o == 1:
            to_near(z, 1, 1, 0)
            to_core(z, 0, 1, 0)
            layer_out[...] = (hidden * gate).astype(BF)
            layer_copy.start()
            w_term[...] = (
                lax.dot_general(summed, hidden_grad, (((0,), (0,)), ((), ())), preferred_element_type=F32)
                * (n_row * n_col * 128) ** (-0.5)
            ).reshape(w_term.shape)
            from_near(z, 0, 1, 0)

    def gath_block(at, o, s, d):
        if o == 0 and d < HZ:
            to_near(at, 1, s, d)
        to_core(at, o, s, d)

    last_sem = fresh()

    def backward_chunk(at):
        product = lax.dot_general(
            dense[pl.ds(pl.multiple_of(at * chunk, chunk), chunk), :],
            gath[at].reshape(chunk, width),
            (((0,), (0,)), ((), ())),
            preferred_element_type=F32,
        )
        return product

    def accumulate(keys, at, start=False):
        for p, s, d in keys:
            arrived(piece(at, p, 1 - k), pair_sems[p, s, d])
        if start:
            acc[...] = backward_chunk(at)
        else:
            acc[...] += backward_chunk(at)

    def weight_steps():
        sem = fresh()
        send(w_term.at[1 - k], w_core, sem, core_dev)
        yield
        arrived(w_core, sem)
        add_into(w_core, w_term.at[k])
        total = yield from ring_sum(
            y, Y, lambda at, o: w_core.at[at, o], wy_p, wy_m, y_plus, y_minus
        )
        for o in (0, 1):
            w_y[o] = total(o).reshape(w_y.shape[1:])
        total = yield from ring_sum(
            x, X, lambda at, o: w_y.at[at // 2, at % 2, o], wx_p, wx_m, x_plus, x_minus
        )
        for o in (0, 1):
            w_z[z, o] = total(o)
        yield from ring_gather(z, Z, lambda at, o: w_z.at[at, o], z_plus, z_minus)
        full = w_z[0]
        for at in range(1, Z):
            full = full + w_z[at]
        w_x[k, y, x] = full
        yield from ring_gather(x, X, lambda at, o: w_x.at[k, y, at, o], x_plus, x_minus)
        yield from ring_gather(
            y, Y, lambda at, o: w_x.at[k, at, pl.ds(o * (X // 2), X // 2)], y_plus, y_minus
        )
        sem = fresh()
        send(w_x.at[k], w_x.at[k], sem, core_dev)
        yield
        arrived(w_x.at[1 - k], sem)

    weight_run = weight_steps()

    def weight_step(count):
        for _ in range(count):
            next(weight_run, None)

    gather_run = ring_gather(
        z, Z, lambda at, o: piece(at, o, k), z_plus, z_minus, ready=gath_ready, on_block=gath_block
    )
    next(gather_run)
    to_core(z, 1, 1, 0)
    weight_step(1)
    from_near(z, 1, 1, 0)
    to_core(z, 2, 1, 0)
    weight_step(1)
    for d in range(1, HZ + 1):
        next(gather_run, None)
        if d == 1:
            accumulate([(p, 1, 0) for p in range(3)], z, start=True)
        else:
            for s in (1, -1):
                accumulate([(p, s, d - 1) for p in range(3)], (z - s * (d - 1) + Z) % Z)
        if d < HZ:
            for s in (-1, 1):
                at = (z - s * d + Z) % Z
                from_near(at, 1, s, d)
                if d == HZ - 1 and s == -1:
                    send(piece(at, 2, k), piece(at, 2, k), last_sem, z_minus)
                to_core(at, 2, s, d)
        weight_step(2)
    far = (z + HZ) % Z
    arrived(piece(far, 2, k), last_sem)
    to_core(far, 2, -1, HZ)
    accumulate([(0, 1, HZ), (1, -1, HZ), (2, -1, HZ)], far)

    back[...] = acc[...].astype(BF).reshape(back.shape)

    def back_at(at, o):
        return back.at[xh if o == 0 else 1 - xh, at]

    steps = ring_sum(y, Y, back_at, yp, ym, y_plus, y_minus)
    while True:
        try:
            next(steps)
            weight_step(1)
        except StopIteration as stop:
            total = stop.value
            break
    far_back = fresh()
    own_sum2 = yp.at[1, 1]
    own_sum2[...] = total(1).astype(BF)
    send(own_sum2, xb_in, far_back, x_far)
    mine = total(0)
    for _ in weight_run:
        pass
    weight_grad_copy = pltpu.make_async_copy(w_x, weight_grad_hbm.reshape(w_x.shape), local_sems.at[4])
    weight_grad_copy.start()
    arrived(xb_in, far_back)
    feat_grad[...] = (mine + xb_in[...].astype(F32)).astype(BF)
    feat_grad_copy = pltpu.make_async_copy(feat_grad, feat_grad_hbm.at[0], local_sems.at[5])
    feat_grad_copy.start()
    for copy in pending:
        copy.wait_send()
    layer_copy.wait()
    weight_grad_copy.wait()
    feat_grad_copy.wait()
    assert counters["send"] <= send_sems.shape[0] and counters["recv"] <= recv_sems.shape[0]


def write_outputs(
    layer_out, feat_grad, weight_grad, layer_hbm, feat_grad_hbm, weight_grad_hbm, layer_buf, feat_grad_buf, weight_buf, sems
):
    rows = weight_buf.shape[0] // 4
    jobs = [(feat_grad, feat_grad_buf, feat_grad_hbm), (layer_out, layer_buf, layer_hbm)]
    for i in range(4):
        at = pl.ds(i * rows, rows)
        jobs.append((weight_grad.at[at], weight_buf.at[at], weight_grad_hbm.at[at]))
    reads = [pltpu.make_async_copy(src, buf, sems.at[0, i]) for i, (src, buf, _) in enumerate(jobs)]
    writes = [pltpu.make_async_copy(buf, dst, sems.at[1, i]) for i, (_, buf, dst) in enumerate(jobs)]
    for read in reads:
        read.start()
    for read, write in zip(reads, writes):
        read.wait()
        write.start()
    for write in writes:
        write.wait()


def local(n_row, n_col, feats, weight, cotangent, tile_values, tile_rows, tile_cols, tile_count):
    rows_here, width = feats.shape[1:]
    slots = tile_values.shape[2]
    Y, Z, X = n_row // X_HI, n_col // (X_LO * CORE), X_HI * X_LO
    row_tiles, col_tiles = n_col, n_row
    ids = tile_rows[0, 0] * col_tiles + tile_cols[0, 0]
    slot_ids = jnp.arange(slots, dtype=jnp.int32)
    ids = jnp.where(slot_ids < tile_count[0, 0], ids, -1)
    places = jnp.arange(row_tiles * col_tiles, dtype=jnp.int32)
    hit = ids[None, :] == places[:, None]
    tab = jnp.min(jnp.where(hit, slot_ids[None, :], slots), axis=1)

    block = (128, width)
    w_rows = width // (CORE * Y * X)
    w_full = (CORE, Y, X, 2, w_rows // 2, width)
    scratch = [
        pltpu.VMEM((width, width), BF),
        pltpu.VMEM(block, BF),
        pltpu.VMEM(block, BF),
        pltpu.VMEM(block, BF),
        pltpu.VMEM((slots + 1, 128, 128), BF),
        pltpu.VMEM((row_tiles * 128, col_tiles * 128), BF),
        pltpu.VMEM((n_row,) + block, BF),
        pltpu.VMEM((Z, X_LO, CORE) + block, BF),
        pltpu.VMEM((Z, X_LO) + block, BF),
        pltpu.VMEM((Z // 2, 2) + block, BF),
        pltpu.VMEM((Z // 2, 2) + block, BF),
        pltpu.VMEM(block, BF),
        pltpu.VMEM(block, BF),
        pltpu.VMEM((Z, X_LO, CORE) + block, BF),
        pltpu.VMEM((col_tiles * 128, width), F32),
        pltpu.VMEM((X_HI, Y) + block, BF),
        pltpu.VMEM((Y // 2, 2) + block, BF),
        pltpu.VMEM((Y // 2, 2) + block, BF),
        pltpu.VMEM(block, BF),
        pltpu.VMEM((CORE, Y, 2, X * w_rows // 2, width), F32),
        pltpu.VMEM((Y, 2, X * w_rows // 2, width), F32),
        pltpu.VMEM((Y // 2, 2, X * w_rows // 2, width), F32),
        pltpu.VMEM((Y // 2, 2, X * w_rows // 2, width), F32),
        pltpu.VMEM((2, X // 2, 2, w_rows // 2, width), F32),
        pltpu.VMEM((X // 2, 2, w_rows // 2, width), F32),
        pltpu.VMEM((X // 2, 2, w_rows // 2, width), F32),
        pltpu.VMEM(w_full, F32),
        pltpu.VMEM((Z, 2, w_rows // 2, width), F32),
        pltpu.SemaphoreType.DMA,
        pltpu.SemaphoreType.DMA((6,)),
        pltpu.SemaphoreType.DMA((180,)),
        pltpu.SemaphoreType.DMA((210,)),
        pltpu.SemaphoreType.DMA((Z,)),
        pltpu.SemaphoreType.DMA((Z,)),
    ]
    hbm = pl.BlockSpec(memory_space=pltpu.HBM)
    layer_out, feat_grad, weight_grad = pl.pallas_call(
        functools.partial(layer_kernel, n_row, n_col),
        out_shape=(
            jax.ShapeDtypeStruct((1,) + block, BF),
            jax.ShapeDtypeStruct((1,) + block, BF),
            jax.ShapeDtypeStruct((width, width), F32),
        ),
        in_specs=[pl.BlockSpec(memory_space=pltpu.SMEM), hbm, hbm, hbm, hbm],
        out_specs=(hbm, hbm, hbm),
        scratch_shapes=scratch,
        compiler_params=pltpu.CompilerParams(
            collective_id=0, has_side_effects=True, vmem_limit_bytes=60 * 1024 * 1024
        ),
    )(tab, feats, weight, cotangent, tile_values)
    return pl.pallas_call(
        write_outputs,
        out_shape=(
            jax.ShapeDtypeStruct((1,) + block, BF),
            jax.ShapeDtypeStruct((1,) + block, BF),
            jax.ShapeDtypeStruct((width, width), F32),
        ),
        in_specs=[hbm, hbm, hbm],
        out_specs=(hbm, hbm, hbm),
        scratch_shapes=[
            pltpu.VMEM((1,) + block, BF),
            pltpu.VMEM((1,) + block, BF),
            pltpu.VMEM((width, width), F32),
            pltpu.SemaphoreType.DMA((2, 6)),
        ],
    )(layer_out, feat_grad, weight_grad)


def solution(mesh):
    in_specs = (
        P("col", "row", None),
        P(),
        P("row", "col", None),
        P("row", "col", None, None, None),
        P("row", "col", None),
        P("row", "col", None),
        P("row", "col"),
    )
    out_specs = (P("row", "col", None), P("col", "row", None), P())
    return jax.shard_map(
        functools.partial(local, mesh.shape["row"], mesh.shape["col"]),
        mesh=mesh, in_specs=in_specs, out_specs=out_specs, check_vma=False,
    )
```
